32 devices in a mesh: leaf: 4 (over z), row: 2 (over y), col: 4 (over x, core).
Axes of the slice: x: 2, y: 2, z: 4, core: 2. Of those that a mesh axis runs over, the one named last changes fastest.
Arguments:
- rhs_root: bfloat16 [64, 4, 768], P('col', None, ('leaf', 'row')), may hold values from -6 to 6
- rhs_child: bfloat16 [64, 4, 768], P('col', None, ('leaf', 'row')), may hold values from -6 to 6
- subtree_update: bfloat16 [64, 4, 1024], P('col', None, ('leaf', 'row')), may hold values from -6 to 6
- inv_root: bfloat16 [4, 768, 3072], P(None, ('leaf', 'row'), 'col'), as said below
- inv_child: bfloat16 [4, 768, 1536], P(None, ('leaf', 'row'), 'col'), as said below
- off_child: bfloat16 [4, 1024, 1536], P(None, ('leaf', 'row'), 'col'), may hold values from -0.15625 to 0.15625
- child_map: int32 [2, 16], replicated, may hold values from 0 to 23, as said below
- subtree_map: int32 [4, 8], replicated, may hold values from 0 to 27, as said below
Outputs:
- solution_root: float32 [64, 4, 768], P('col', None, ('leaf', 'row'))
- solution_child: float32 [64, 4, 768], P('col', None, ('leaf', 'row'))
- leaf_solution: bfloat16 [64, 4, 1024], P('col', None, ('leaf', 'row'))
The draws below stay inside these ranges and needn't reach their ends.
Inputs may be any that keep to these rules, and one draw needn't show every extreme that they name: `child_map`: each row names 16 different blocks. `subtree_map`: each row names 8 different blocks. `inv_root`: zero above the diagonal, positive on it. `inv_child`: each child's block is zero above the diagonal, positive on it.
All inputs are finite; a program needn't handle non-finite values.
Results may differ from the reference program's by a relative error of at most 0.017.
Values may be sent and summed in bfloat16 or wider, within the bound.
A program may use at most 64 MiB of HBM per device.

```python
import math
import jax
import jax.numpy as jnp
from jax import lax

RIGHT_SIDES = 64
BLOCK_ROWS = 128
ROOT_ORDER = 3072
CHILD_ORDER = 1536
CHILD_UPDATE = 2048
SUBTREE_UPDATE = 1024
ROOT_BLOCKS = 24
CHILD_BLOCKS = 28
UPDATE_BLOCKS = 16
SUBTREE_BLOCKS = 8
N_COL = 4


def triangle(key, row_number, column_number, order):
    first_key, second_key = jax.random.split(key)
    extent = row_number.shape
    spread = jnp.clip(jax.random.normal(first_key, extent, jnp.float32), -6.0, 6.0)
    diagonal = jax.random.uniform(second_key, extent, jnp.float32, 0.5, 1.5)
    lower_part = spread / math.sqrt(order)
    return jnp.where(column_number < row_number, lower_part, jnp.where(column_number == row_number, diagonal, 0.0))


def draw_inv_root(key, part):
    extent = (N_COL, ROOT_ORDER // N_COL, ROOT_ORDER)
    quarter = lax.broadcasted_iota(jnp.int32, extent, 0)
    within = lax.broadcasted_iota(jnp.int32, extent, 1)
    column_number = lax.broadcasted_iota(jnp.int32, extent, 2)
    row_number = quarter * (ROOT_ORDER // N_COL) + within
    return triangle(key, row_number, column_number, ROOT_ORDER).astype(jnp.bfloat16)


def draw_inv_child(key, part):
    extent = (N_COL, 2 * CHILD_ORDER // N_COL, CHILD_ORDER)
    quarter = lax.broadcasted_iota(jnp.int32, extent, 0)
    within = lax.broadcasted_iota(jnp.int32, extent, 1) % (CHILD_ORDER // N_COL)
    column_number = lax.broadcasted_iota(jnp.int32, extent, 2)
    row_number = quarter * (CHILD_ORDER // N_COL) + within
    return triangle(key, row_number, column_number, CHILD_ORDER).astype(jnp.bfloat16)


def block_table(key, table_rows, width_blocks, limit):
    table = []
    for number in range(table_rows):
        row_key = jax.random.fold_in(key, number)
        if number == 0:
            middle = 1 + jax.random.permutation(row_key, limit - 2)[:width_blocks - 2]
            edges = jnp.array([0, limit - 1], dtype=jnp.int32)
            entries = jax.random.permutation(jax.random.fold_in(row_key, 101), jnp.concatenate([edges, middle.astype(jnp.int32)]))
        else:
            entries = jax.random.permutation(row_key, limit)[:width_blocks]
        table.append(entries.astype(jnp.int32))
    return jnp.stack(table)


def draw_child_map(key, part):
    return block_table(key, 2, UPDATE_BLOCKS, ROOT_BLOCKS)


def draw_subtree_map(key, part):
    return block_table(key, 4, SUBTREE_BLOCKS, CHILD_BLOCKS)


def level_of(own_key, shape, cuts, low, top_value):
    level = 1.0
    for position, blocks in cuts:
        steps = jax.random.uniform(jax.random.fold_in(jax.random.fold_in(own_key, 6), position), (blocks,), jnp.float32, low / len(cuts), top_value / len(cuts))
        level = level * jnp.repeat(jnp.exp(steps), shape[position] // blocks).reshape((-1,) + (1,) * (len(shape) - 1 - position))
    return level


def gaussian(own_key, shape, deviation, most, cuts=(), held_as=jnp.bfloat16):
    level = level_of(own_key, shape, cuts, -0.22, 0.18) if cuts else 1.0
    values = jax.random.normal(own_key, shape, jnp.float32) * deviation * level
    return jnp.minimum(jnp.maximum(values, -most), most).astype(held_as)


def setup_inputs(seed: int = 0) -> dict:
    seeds = jax.random.split(jax.random.key(seed), 9)
    return {
        "rhs_root": gaussian(seeds[0], (RIGHT_SIDES, N_COL, ROOT_ORDER // N_COL), 1.0, 6.0, ((0, 4), (2, 8))),
        "rhs_child": gaussian(seeds[1], (RIGHT_SIDES, N_COL, 2 * CHILD_ORDER // N_COL), 1.0, 6.0, ((0, 4), (2, 8))),
        "subtree_update": gaussian(seeds[2], (RIGHT_SIDES, N_COL, 4 * SUBTREE_UPDATE // N_COL), 1.0, 6.0, ((0, 4), (2, 8))),
        "inv_root": draw_inv_root(jax.random.fold_in(seeds[8], 71), 0),
        "inv_child": draw_inv_child(jax.random.fold_in(seeds[8], 71), 0),
        "off_child": gaussian(seeds[5], (N_COL, 2 * CHILD_UPDATE // N_COL, CHILD_ORDER), CHILD_ORDER ** -0.5, 0.15625, ((1, 8), (2, 4))),
        "child_map": draw_child_map(jax.random.fold_in(seeds[8], 71), 0),
        "subtree_map": draw_subtree_map(jax.random.fold_in(seeds[8], 71), 0),
    }


def add_blocks(front_vector, update, block_map):
    right_sides = front_vector.shape[0]
    blocks = front_vector.reshape(right_sides, -1, BLOCK_ROWS)
    pieces = update.astype(jnp.float32).reshape(right_sides, -1, BLOCK_ROWS)
    return blocks.at[:, block_map, :].add(pieces).reshape(right_sides, -1)


def pick_blocks(front_vector, block_map):
    right_sides = front_vector.shape[0]
    return front_vector.reshape(right_sides, -1, BLOCK_ROWS)[:, block_map, :].reshape(right_sides, -1)


def unpack_vectors(packed, fronts):
    right_sides, tile_count, length = packed.shape
    return packed.reshape(right_sides, tile_count, fronts, length // fronts).transpose(2, 0, 1, 3).reshape(fronts, right_sides, -1)


def pack_vectors(stacked):
    fronts, right_sides, length = stacked.shape
    return stacked.reshape(fronts, right_sides, N_COL, length // N_COL).transpose(1, 2, 0, 3).reshape(right_sides, N_COL, -1)


def unpack_blocks(packed, fronts):
    tile_count, height, columns_all = packed.shape
    return packed.reshape(tile_count, fronts, height // fronts, columns_all).transpose(1, 0, 2, 3).reshape(fronts, -1, columns_all)


def reference(rhs_root, rhs_child, subtree_update, inv_root, inv_child, off_child, child_map, subtree_map):
    root_order = inv_root.shape[2]
    child_order = inv_child.shape[2]
    root_matrix = inv_root.reshape(root_order, root_order)
    child_matrices = unpack_blocks(inv_child, 2)
    off_matrices = unpack_blocks(off_child, 2)
    child_update = off_matrices.shape[1]
    right_sides = rhs_root.shape[0]
    child_rhs = unpack_vectors(rhs_child, 2)
    subtree_vectors = unpack_vectors(subtree_update, 4)
    forwards = []
    passes = []
    for front_number in range(2):
        front_vector = jnp.concatenate([child_rhs[front_number].astype(jnp.float32), jnp.zeros((right_sides, child_update), jnp.float32)], 1)
        for half_number in range(2):
            subtree_number = 2 * front_number + half_number
            front_vector = add_blocks(front_vector, subtree_vectors[subtree_number], subtree_map[subtree_number])
        separator = front_vector[:, :child_order].astype(jnp.bfloat16)
        forward = jnp.dot(separator, child_matrices[front_number].T, preferred_element_type=jnp.float32).astype(jnp.bfloat16)
        passed = (front_vector[:, child_order:] - jnp.dot(forward, off_matrices[front_number].T, preferred_element_type=jnp.float32)).astype(jnp.bfloat16)
        forwards.append(forward)
        passes.append(passed)
    root_vector = rhs_root.reshape(right_sides, root_order).astype(jnp.float32)
    for front_number in range(2):
        root_vector = add_blocks(root_vector, passes[front_number], child_map[front_number])
    root_forward = jnp.dot(root_vector.astype(jnp.bfloat16), root_matrix.T, preferred_element_type=jnp.float32).astype(jnp.bfloat16)
    solution_root = jnp.dot(root_forward, root_matrix, preferred_element_type=jnp.float32)
    root_rounded = solution_root.astype(jnp.bfloat16)
    solutions = []
    leaves = []
    for front_number in range(2):
        known_rows = pick_blocks(root_rounded, child_map[front_number])
        backward = (forwards[front_number].astype(jnp.float32) - jnp.dot(known_rows, off_matrices[front_number], preferred_element_type=jnp.float32)).astype(jnp.bfloat16)
        solution = jnp.dot(backward, child_matrices[front_number], preferred_element_type=jnp.float32)
        whole_front = jnp.concatenate([solution.astype(jnp.bfloat16), known_rows], 1)
        solutions.append(solution)
        for half_number in range(2):
            leaves.append(pick_blocks(whole_front, subtree_map[2 * front_number + half_number]))
    return (solution_root.reshape(right_sides, N_COL, root_order // N_COL), pack_vectors(jnp.stack(solutions)), pack_vectors(jnp.stack(leaves)))
```

```python
import functools

import jax
import jax.numpy as jnp
from jax import lax
from jax.experimental import pallas as pl
from jax.experimental.pallas import tpu as pltpu
from jax.sharding import PartitionSpec as P

BLOCK_ROWS = 128


def partner_2(block, axis, bit):
    count = lax.axis_size(axis)
    route = []
    for low in range(count):
        high = low | 1 << bit
        if high != low and high < count:
            route += [(low, high), (high, low)]
    return lax.ppermute(block, axis, route)


def group_gather(piece, group_size):
    merged = lax.all_gather(piece, "row", axis=2, tiled=True)
    leaf_index = lax.axis_index("leaf")
    for bit_number in range(group_size.bit_length() - 1):
        partner = partner_2(merged, "leaf", bit_number)
        upper = leaf_index >> bit_number & 1 == 1
        merged = jnp.where(
            upper, jnp.concatenate([partner, merged], 2), jnp.concatenate([merged, partner], 2)
        )
    return merged


def group_sum(partial_sum, group_size):
    leaf_index = lax.axis_index("leaf")
    for bit_number in reversed(range(group_size.bit_length() - 1)):
        middle = partial_sum.shape[1] // 2
        lower_half = partial_sum[:, :middle]
        upper_half = partial_sum[:, middle:]
        upper = leaf_index >> bit_number & 1 == 1
        outgoing = jnp.where(upper, lower_half, upper_half)
        kept_half = jnp.where(upper, upper_half, lower_half)
        partial_sum = kept_half + partner_2(
            outgoing.astype(jnp.bfloat16), "leaf", bit_number
        ).astype(outgoing.dtype)
    return lax.psum_scatter(
        partial_sum.astype(jnp.bfloat16), "row", scatter_dimension=1, tiled=True
    ).astype(jnp.float32)


def one_hot(block_map, blocks_total):
    return (block_map[..., None] == jnp.arange(blocks_total, dtype=jnp.int32)).astype(jnp.bfloat16)


def pick_piece(source, position, along):
    return lax.dynamic_index_in_dim(source, position, along, keepdims=False)


def contract(left_side, right_side, left_dim, right_dim):
    return lax.dot_general(
        left_side,
        right_side,
        (((left_dim,), (right_dim,)), ((), ())),
        preferred_element_type=jnp.float32,
    )


def local(
    rhs_root, rhs_child, subtree_update, inv_root, inv_child, off_child, child_map, subtree_map
):
    n_col = lax.axis_size("col")
    n_row = lax.axis_size("row")
    n_leaf = lax.axis_size("leaf")
    group_size = n_leaf // 2
    sub_size = n_leaf // 4
    col_index = lax.axis_index("col")
    leaf_index = lax.axis_index("leaf")
    row_index = lax.axis_index("row")
    front_index = leaf_index // group_size
    member = leaf_index % group_size
    child_rank = member * n_row + row_index
    half_index = member // sub_size
    sub_rank = member % sub_size * n_row + row_index
    panel_width = rhs_child.shape[0]
    right_sides = panel_width * n_col
    sep_piece = rhs_child.shape[2]
    upd_piece = subtree_update.shape[2]
    root_width = inv_root.shape[2]
    child_width = inv_child.shape[2]
    child_order = child_width * n_col
    child_update = upd_piece * n_col * group_size * n_row
    root_blocks = root_width * n_col // BLOCK_ROWS
    child_blocks = (child_order + child_update) // BLOCK_ROWS
    root_matrix = inv_root.reshape(n_col * sep_piece, root_width)
    child_matrix = inv_child.reshape(n_col * sep_piece, child_width)
    off_matrix = off_child.reshape(n_col * upd_piece, child_width)
    joined = jnp.concatenate([subtree_update, rhs_child], 2)
    gathered = group_gather(joined, group_size).reshape(
        panel_width, n_col, group_size * n_row, upd_piece + sep_piece
    )
    sub_vectors = (
        gathered[..., :upd_piece]
        .reshape(panel_width, n_col, 2, -1)
        .transpose(2, 0, 1, 3)
        .reshape(2, panel_width, -1, BLOCK_ROWS)
    )
    child_rhs_full = gathered[..., upd_piece:].reshape(panel_width, child_order)
    sub_rows = lax.dynamic_slice_in_dim(subtree_map, 2 * front_index, 2, 0)
    spread = jnp.einsum(
        "hpjt,hjn->pnt",
        sub_vectors,
        one_hot(sub_rows, child_blocks),
        preferred_element_type=jnp.float32,
    ).reshape(panel_width, -1)
    child_sep = (spread[:, :child_order] + child_rhs_full.astype(jnp.float32)).astype(jnp.bfloat16)
    child_tail = spread[:, child_order:]
    child_tile = lax.all_to_all(
        child_sep.reshape(panel_width, n_col, child_width),
        "col",
        split_axis=1,
        concat_axis=0,
        tiled=True,
    ).reshape(right_sides, child_width)
    child_forward = lax.psum(contract(child_tile, child_matrix, 1, 1), "col").astype(jnp.bfloat16)
    forward_quarter = lax.dynamic_slice_in_dim(
        child_forward.reshape(right_sides, n_col, sep_piece), col_index, 1, 1
    )
    forward_tile = group_gather(forward_quarter, group_size).reshape(right_sides, child_width)
    pass_term = lax.psum_scatter(
        contract(forward_tile, off_matrix, 1, 1), "col", scatter_dimension=0, tiled=True
    )
    tail_mine = pick_piece(
        child_tail.reshape(panel_width, n_col, group_size * n_row, upd_piece), child_rank, 2
    )
    child_pass = (tail_mine - pass_term.reshape(panel_width, n_col, upd_piece)).astype(jnp.bfloat16)
    joined_root = jnp.concatenate([child_pass, rhs_root], 2)
    root_all = lax.all_gather(joined_root, ("leaf", "row"), axis=2, tiled=True).reshape(
        panel_width, n_col, n_leaf * n_row, upd_piece + sep_piece
    )
    pass_vectors = (
        root_all[..., :upd_piece]
        .reshape(panel_width, n_col, 2, -1)
        .transpose(2, 0, 1, 3)
        .reshape(2, panel_width, -1, BLOCK_ROWS)
    )
    root_rhs_full = root_all[..., upd_piece:].reshape(panel_width, root_width * n_col)
    root_spread = jnp.einsum(
        "hpjt,hjn->pnt",
        pass_vectors,
        one_hot(child_map, root_blocks),
        preferred_element_type=jnp.float32,
    ).reshape(panel_width, -1)
    root_sep = (root_spread + root_rhs_full.astype(jnp.float32)).astype(jnp.bfloat16)
    root_tile = lax.all_to_all(
        root_sep.reshape(panel_width, n_col, root_width),
        "col",
        split_axis=1,
        concat_axis=0,
        tiled=True,
    ).reshape(right_sides, root_width)
    root_forward = lax.psum(contract(root_tile, root_matrix, 1, 1), "col").astype(jnp.bfloat16)
    map_row = pick_piece(child_map, front_index, 0)
    root_piece = lax.psum_scatter(
        contract(root_matrix, root_forward, 0, 1), ("leaf", "row"), scatter_dimension=0, tiled=True
    )
    solution_root = lax.all_to_all(
        root_piece.T.reshape(right_sides, 1, sep_piece),
        "col",
        split_axis=0,
        concat_axis=1,
        tiled=True,
    )
    root_everywhere = lax.all_gather(
        solution_root.astype(jnp.bfloat16), ("leaf", "row"), axis=2, tiled=True
    ).reshape(panel_width, root_blocks, BLOCK_ROWS)
    known_full = (
        jnp.einsum(
            "pnt,jn->pjt",
            root_everywhere,
            one_hot(map_row, root_blocks),
            preferred_element_type=jnp.float32,
        )
        .astype(jnp.bfloat16)
        .reshape(panel_width, child_update)
    )
    known_mine = pick_piece(
        known_full.reshape(panel_width, n_col, group_size * n_row, upd_piece), child_rank, 2
    )
    known_rows = lax.all_gather(known_mine, "col", axis=0, tiled=True).reshape(
        right_sides, n_col * upd_piece
    )
    correction = group_sum(contract(known_rows, off_matrix, 1, 0), group_size)
    back_quarter = (
        forward_quarter.reshape(right_sides, sep_piece).astype(jnp.float32) - correction
    ).astype(jnp.bfloat16)
    back_rows = lax.all_gather(
        back_quarter.reshape(right_sides, 1, sep_piece), "col", axis=1, tiled=True
    ).reshape(right_sides, n_col * sep_piece)
    child_piece = group_sum(contract(back_rows, child_matrix, 1, 0), group_size)
    solution_child = lax.all_to_all(
        child_piece.reshape(right_sides, 1, sep_piece),
        "col",
        split_axis=0,
        concat_axis=1,
        tiled=True,
    )
    child_rounded = solution_child.astype(jnp.bfloat16)
    sep_whole = group_gather(child_rounded, group_size).reshape(panel_width, child_order)
    child_whole = jnp.concatenate([sep_whole, known_full], 1)
    sub_row = pick_piece(subtree_map, 2 * front_index + half_index, 0)
    leaf_full = jnp.einsum(
        "pnt,jn->pjt",
        child_whole.reshape(panel_width, child_blocks, BLOCK_ROWS),
        one_hot(sub_row, child_blocks),
        preferred_element_type=jnp.float32,
    ).astype(jnp.bfloat16)
    leaf_solution = pick_piece(
        leaf_full.reshape(panel_width, n_col, sub_size * n_row, upd_piece), sub_rank, 2
    )
    return (solution_root, solution_child, leaf_solution)


F32 = jnp.float32
BF16 = jnp.bfloat16


def add_up(terms):
    total = terms[0]
    for term in terms[1:]:
        total = total + term
    return total


def solve_kernel(
    child_hbm_map, subtree_hbm_map, sub_hbm, rc_hbm, rr_hbm, root_hbm, child_hbm, off_hbm,
    root_out, child_out, leaf_out,
    child_map, subtree_map, sub_in, rc_in, rr_in,
    root_w, child_w, off_w,
    rhs_send, rhs_recv, rr_send, rr_buf,
    fwd_send, fwd_recv, half_send, half_recv, half_own, forward_own,
    pass_send, pass_buf, root_x, solved,
    known_send, known_recv, extra_send, extra_recv,
    back_send, back_recv, final_blocks, final_send, final_recv,
    load_sems, send_sems, recv_sems, share_sems, shared_sems,
):
    n_leaf, n_row, n_col = lax.axis_size("leaf"), lax.axis_size("row"), lax.axis_size("col")
    panel = sub_in.shape[0]
    sep = rc_in.shape[2]
    ranks = n_row * (n_leaf // 2)
    rows_all = n_leaf * n_row
    child_tile_blocks = child_w.shape[3] // BLOCK_ROWS
    root_tile_blocks = root_w.shape[3] // BLOCK_ROWS
    sep_blocks = child_tile_blocks * n_col
    piece_blocks = n_col * sep // BLOCK_ROWS
    c = lax.axis_index("col")
    leaf = lax.axis_index("leaf")
    row = lax.axis_index("row")
    x = lax.div(c, 2)
    core = lax.rem(c, 2)
    front = lax.div(leaf, 2)
    low = lax.rem(leaf, 2)
    rank = low * n_row + row
    r = leaf * n_row + row
    pair = 2 * x + 1 - core
    across = 2 * (1 - x) + core
    far = 2 * (1 - x) + 1 - core

    loads = [
        pltpu.make_async_copy(source, target, load_sems.at[number])
        for number, (source, target) in enumerate((
            (sub_hbm, sub_in), (rc_hbm, rc_in),
            (subtree_hbm_map, subtree_map), (child_hbm_map, child_map),
            (child_hbm, child_w.at[c]), (root_hbm, root_w.at[c]),
            (off_hbm, off_w.at[c]), (rr_hbm, rr_in),
        ))
    ]
    for load in loads:
        load.start()

    def flip(m):
        other_leaf = 2 * (1 - front if m & 4 else front) + (1 - low if m & 2 else low)
        other_row = 1 - row if m & 1 else row
        return {"leaf": other_leaf, "row": other_row}, other_leaf * n_row + other_row

    def at(m, c2):
        place, _ = flip(m)
        return {**place, "col": c2}

    def push(source, target, phase, device):
        pltpu.make_async_remote_copy(
            src_ref=source,
            dst_ref=target,
            send_sem=send_sems.at[phase],
            recv_sem=recv_sems.at[phase],
            device_id=device,
            device_id_type=pl.DeviceIdType.MESH,
        ).start()

    def drain(view, sem):
        pltpu.make_async_copy(view, view, sem).wait()

    barrier = pltpu.get_barrier_semaphore()

    def greet(device):
        pl.semaphore_signal(
            barrier, inc=1, device_id=device, device_id_type=pl.DeviceIdType.MESH
        )

    def tiles_of(full, c2, body):
        for q in (3, 2, 1, 0):
            if full:
                body(q)
            else:
                pl.when(q >= c2)(functools.partial(body, q))

    def hand(weights, slot, q, number, kind, c2):
        pltpu.make_async_remote_copy(
            src_ref=weights.at[slot, q],
            dst_ref=weights.at[slot, q],
            send_sem=share_sems.at[number, kind, q],
            recv_sem=shared_sems.at[number, kind, q],
            device_id={"leaf": leaf, "row": row, "col": c2},
            device_id_type=pl.DeviceIdType.MESH,
        ).start()

    def share_across(weights, number):
        tiles_of(number == 1, c, lambda q: hand(weights, c, q, number, 0, across))

    def share_pair(weights, number):
        tiles_of(number < 2, c, lambda q: hand(weights, c, q, number, 1, pair))

    def settle_pair(weights, number):
        tiles_of(number < 2, pair, lambda q: drain(weights.at[0, q], shared_sems.at[number, 1, q]))

    def relay(weights, number):
        def pass_on(q):
            drain(weights.at[across, q], shared_sems.at[number, 0, q])
            hand(weights, across, q, number, 2, pair)

        tiles_of(number == 1, across, pass_on)

    def settle_far(weights, number):
        tiles_of(number == 1, far, lambda q: drain(weights.at[0, q], shared_sems.at[number, 2, q]))

    def conclude(weights, number, kind, slot):
        full = number == 1 or (number == 0 and kind == 1)
        tiles_of(full, slot, lambda q: drain(weights.at[0, q], share_sems.at[number, kind, q]))

    def lower(weights, c2):
        return weights[c2, c2:].reshape(-1, weights.shape[3])

    def flat(weights, c2):
        return weights[c2].reshape(-1, weights.shape[3])

    for m in range(rows_all):
        if m > 0:
            greet(at(m, c))
        greet(at(m, across))
    greet(at(0, pair))

    loads[0].wait()
    loads[1].wait()
    pad = jnp.zeros((panel, BLOCK_ROWS - sep), BF16)
    for q in range(n_col):
        value = sub_in[:, q, :]
        for half in range(2):
            rhs_send[half, q] = value
        rhs_send[q // 2, n_col + q % 2] = jnp.concatenate([rc_in[:, q, :], pad], 1)
    rhs_width = rhs_send.shape[1]
    group = 2 * ranks
    no_rhs = group * rhs_width
    no_pass = 2 * rows_all * n_col
    rhs_recv[no_rhs] = jnp.zeros((panel, BLOCK_ROWS), BF16)
    pass_buf[no_pass] = jnp.zeros((panel, BLOCK_ROWS), BF16)
    pl.semaphore_wait(barrier, 2 * rows_all)

    for side in (1, 0):
        for m in reversed(range(ranks)):
            if side or m:
                half = 1 - x if side else x
                push(
                    rhs_send.at[half],
                    rhs_recv.at[pl.ds((x * ranks + rank) * rhs_width, rhs_width)],
                    0,
                    at(m, across if side else c),
                )
    rhs_recv[pl.ds((x * ranks + rank) * rhs_width, rhs_width)] = rhs_send[x]
    loads[4].wait()
    share_pair(child_w, 0)
    loads[5].wait()

    @pl.when(x == 0)
    def _():
        share_pair(root_w, 2)

    @pl.when(x == 1)
    def _():
        share_across(root_w, 2)

    loads[6].wait()
    share_pair(off_w, 1)
    loads[7].wait()
    for q in range(n_col):
        rr_send[q] = rr_in[:, q, :]
    loads[2].wait()
    loads[3].wait()
    targets = [
        [subtree_map[2 * front + h, j] for j in range(subtree_map.shape[1])] for h in range(2)
    ]

    def sub_place(h, block):
        place = -1
        for j, target in enumerate(targets[h]):
            source = (h * n_row + j % n_row) * rhs_width + j // n_row
            place = jnp.where(target == block, source, place)
        return place

    def sub_value(p, place):
        index = jnp.where(place >= 0, p * ranks * rhs_width + place, no_rhs)
        return rhs_recv[index].astype(F32)

    half_places = [
        [[sub_place(h, (2 * x + i) * child_tile_blocks + b) for h in range(2)]
         for b in range(child_tile_blocks)]
        for i in range(2)
    ]
    drain(rhs_recv.at[pl.ds(0, (group - 1) * rhs_width)], recv_sems.at[0])
    settle_pair(child_w, 0)
    partial_sum = None
    for i in range(2):
        rows = []
        for p in range(2):
            rhs = jnp.concatenate(
                [
                    rhs_recv[(p * ranks + k) * rhs_width + n_col + i][:, :sep].astype(F32)
                    for k in range(ranks)
                ],
                1,
            )
            placed = jnp.concatenate(
                [
                    sub_value(p, half_places[i][b][0]) + sub_value(p, half_places[i][b][1])
                    for b in range(child_tile_blocks)
                ],
                1,
            )
            rows.append(rhs + placed)
        term = contract(
            jnp.concatenate(rows, 0).astype(BF16), flat(child_w, 2 * x + i), 1, 1
        )
        partial_sum = term if partial_sum is None else partial_sum + term
    for q in range(n_col):
        fwd_send[q // 2, q % 2] = partial_sum[:, q * sep : (q + 1) * sep].astype(BF16)

    for side in (1, 0):
        for m in reversed(range(ranks)):
            if side or m:
                half = 1 - x if side else x
                push(
                    fwd_send.at[half], fwd_recv.at[x * ranks + rank], 1,
                    at(m, across if side else c),
                )
    fwd_recv[x * ranks + rank] = fwd_send[x]

    @pl.when(x == 0)
    def _():
        share_across(off_w, 1)

    for m in reversed(range(rows_all)):
        if m:
            push(rr_send, rr_buf.at[x * rows_all + r], 2, at(m, core))

    @pl.when(x == 1)
    def _():
        push(rr_send, rr_buf.at[rows_all + r], 2, at(0, core))

    @pl.when(x == 0)
    def _():
        rr_buf[r] = rr_send[...]

    tail = []
    for q in range(n_col):
        block = sep_blocks + q * ranks + rank
        tail.append(sub_value(x, sub_place(0, block)) + sub_value(x, sub_place(1, block)))
    settle_pair(off_w, 1)
    drain(fwd_recv.at[pl.ds(0, group - 1)], recv_sems.at[1])
    z = None
    for i in range(2):
        y = jnp.concatenate(
            [
                fwd_recv[k, i].astype(F32) + fwd_recv[ranks + k, i].astype(F32)
                for k in range(ranks)
            ],
            1,
        ).astype(BF16)
        term = contract(y, flat(off_w, 2 * x + i), 1, 1)
        z = term if z is None else z + term
    for p in range(2):
        for q in range(n_col):
            half_own[p, q] = z[p * panel : (p + 1) * panel, q * BLOCK_ROWS : (q + 1) * BLOCK_ROWS]
    for q in range(n_col):
        half_send[q] = half_own[1 - x, q].astype(BF16)
    for i in range(2):
        mine = (fwd_recv[rank, i].astype(F32) + fwd_recv[ranks + rank, i].astype(F32)).astype(BF16)
        other = jnp.where(x == 0, mine[panel:], mine[:panel])
        half_send[n_col + i] = jnp.concatenate([other, pad], 1)
        forward_own[2 * x + i] = jnp.where(x == 0, mine[:panel], mine[panel:])
    push(half_send, half_recv, 3, at(0, across))

    drain(half_recv, recv_sems.at[3])
    for q in range(n_col):
        total = half_own[x, q] + half_recv[q].astype(F32)
        pass_send[q] = (tail[q] - total).astype(BF16)
    for m in reversed(range(rows_all)):
        if m:
            push(pass_send, pass_buf.at[pl.ds((x * rows_all + r) * n_col, n_col)], 4, at(m, core))

    @pl.when(x == 1)
    def _():
        push(pass_send, pass_buf.at[pl.ds((rows_all + r) * n_col, n_col)], 4, at(0, core))
        share_across(off_w, 1)

    share_across(child_w, 0)
    for i in range(2):
        forward_own[2 * (1 - x) + i] = half_recv[n_col + i][:, :sep]

    @pl.when(x == 0)
    def _():
        pass_buf[pl.ds(r * n_col, n_col)] = pass_send[...]
        maps = [[child_map[f, j] for j in range(child_map.shape[1])] for f in range(2)]

        def pass_place(f, block):
            place = -1
            for j, target in enumerate(maps[f]):
                source = (f * ranks + j % ranks) * n_col + j // ranks
                place = jnp.where(target == block, source, place)
            return place

        places = [
            [pass_place(f, block) for f in range(2)] for block in range(root_tile_blocks * n_col)
        ]
        relay(root_w, 2)
        drain(rr_buf.at[pl.ds(0, 2 * rows_all - 1)], recv_sems.at[2])
        for q in range(n_col):
            root_x[q] = jnp.concatenate(
                [
                    jnp.concatenate(
                        [rr_buf[p * rows_all + k, q].astype(F32) for k in range(rows_all)], 1
                    )
                    for p in range(2)
                ],
                0,
            )
        settle_pair(root_w, 2)
        settle_far(root_w, 2)
        drain(pass_buf.at[pl.ds(0, (2 * rows_all - 1) * n_col)], recv_sems.at[4])

        def pass_value(p, block):
            total = None
            for f in range(2):
                place = places[block][f]
                index = jnp.where(place >= 0, p * rows_all * n_col + place, no_pass)
                value = pass_buf[index].astype(F32)
                total = value if total is None else total + value
            return total

        terms = []
        for c2 in range(n_col):
            passed = jnp.concatenate(
                [
                    jnp.concatenate(
                        [pass_value(p, c2 * root_tile_blocks + b) for b in range(root_tile_blocks)],
                        1,
                    )
                    for p in range(2)
                ],
                0,
            )
            term = contract((root_x[c2] + passed).astype(BF16), lower(root_w, c2), 1, 1)
            if c2 > 0:
                term = jnp.concatenate([jnp.zeros((2 * panel, c2 * sep), F32), term], 1)
            terms.append(term)
        root_forward = add_up(terms)
        totals = []
        for c2 in range(n_col):
            total = contract(
                root_forward[:, c2 * sep :].astype(BF16), lower(root_w, c2), 1, 0
            )
            for b in range(root_tile_blocks):
                solved[c2 * root_tile_blocks + b] = total[
                    :, b * BLOCK_ROWS : (b + 1) * BLOCK_ROWS
                ].astype(BF16)
            totals.append(total)
        for r2 in range(rows_all):
            for q in range(n_col):
                block = solved[child_map[r2 // ranks, q * ranks + r2 % ranks]]
                for p in range(2):
                    known_send[2 * r2 + p, q] = block[p * panel : (p + 1) * panel]
        for m in reversed(range(rows_all)):
            _, r2 = flip(m)
            push(known_send.at[2 * r2 + 1], known_recv.at[r], 5, at(m, across))
            if m:
                push(known_send.at[2 * r2], known_recv.at[r], 5, at(m, c))
        known_recv[r] = known_send[2 * r]
        for r2 in range(rows_all):
            for q in range(n_col):
                block = subtree_map[r2 // n_row, q * n_row + r2 % n_row]
                block = solved[child_map[r2 // ranks, jnp.maximum(block - sep_blocks, 0)]]
                for p in range(2):
                    extra_send[2 * r2 + p, q] = block[p * panel : (p + 1) * panel]
            piece = jnp.concatenate(
                [total[:, r2 * sep : (r2 + 1) * sep] for total in totals], 1
            ).astype(BF16)
            for p in range(2):
                for b in range(piece_blocks):
                    extra_send[2 * r2 + p, n_col + b] = piece[
                        p * panel : (p + 1) * panel, b * BLOCK_ROWS : (b + 1) * BLOCK_ROWS
                    ]
        for m in reversed(range(rows_all)):
            _, r2 = flip(m)
            push(extra_send.at[2 * r2 + 1], extra_recv.at[r], 6, at(m, across))
            if m:
                push(extra_send.at[2 * r2], extra_recv.at[r], 6, at(m, c))
        extra_recv[r] = extra_send[2 * r]

    relay(off_w, 1)
    settle_far(off_w, 1)

    def from_root(buffer, phase):
        pl.when(x == 0)(lambda: drain(buffer.at[pl.ds(0, rows_all - 1)], recv_sems.at[phase]))
        pl.when(x == 1)(lambda: drain(buffer, recv_sems.at[phase]))

    from_root(known_recv, 5)
    known = jnp.concatenate(
        [
            add_up([known_recv[k, q].astype(F32) for k in range(rows_all)])
            for q in range(n_col)
        ],
        1,
    ).astype(BF16)
    corrections = [contract(known, flat(off_w, c2), 1, 0) for c2 in range(n_col)]
    for k in range(ranks):
        back_send[k] = jnp.concatenate(
            [term[:, k * sep : (k + 1) * sep] for term in corrections], 1
        ).astype(BF16)

    def rank_of(m):
        _, r2 = flip(m)
        return r2 - front * ranks

    for m in reversed(range(1, ranks)):
        push(back_send.at[rank_of(m)], back_recv.at[rank], 7, at(m, c))
    back_recv[rank] = back_send[rank]
    relay(child_w, 0)
    own = jnp.concatenate([forward_own[q].astype(F32) for q in range(n_col)], 1)
    settle_far(child_w, 0)
    drain(back_recv.at[pl.ds(0, ranks - 1)], recv_sems.at[7])
    back = own - add_up([back_recv[k].astype(F32) for k in range(ranks)])
    totals = []
    for c2 in range(n_col):
        total = contract(back[:, c2 * sep :].astype(BF16), lower(child_w, c2), 1, 0)
        for b in range(child_tile_blocks):
            final_blocks[c2 * child_tile_blocks + b] = total[
                :, b * BLOCK_ROWS : (b + 1) * BLOCK_ROWS
            ].astype(BF16)
        totals.append(total)
    for k in range(ranks):
        for q in range(n_col):
            block = subtree_map[2 * front + k // n_row, q * n_row + k % n_row]
            final_send[k, q] = final_blocks[jnp.minimum(block, sep_blocks - 1)]
        piece = jnp.concatenate(
            [total[:, k * sep : (k + 1) * sep] for total in totals], 1
        ).astype(BF16)
        for b in range(piece_blocks):
            final_send[k, n_col + b] = piece[:, b * BLOCK_ROWS : (b + 1) * BLOCK_ROWS]
    for m in reversed(range(1, ranks)):
        push(final_send.at[rank_of(m)], final_recv.at[rank], 8, at(m, c))
    final_recv[rank] = final_send[rank]

    def piece_of(buffer, count):
        total = jnp.concatenate(
            [
                add_up([buffer[k, n_col + b].astype(F32) for k in range(count)])
                for b in range(piece_blocks)
            ],
            1,
        )
        return total.reshape(panel, n_col, sep)

    from_root(extra_recv, 6)
    root_out[...] = piece_of(extra_recv, rows_all)
    known_blocks = [
        add_up([extra_recv[k, q].astype(F32) for k in range(rows_all)]) for q in range(n_col)
    ]
    drain(final_recv.at[pl.ds(0, ranks - 1)], recv_sems.at[8])
    child_out[...] = piece_of(final_recv, ranks)
    for q in range(n_col):
        block = subtree_map[leaf, q * n_row + row]
        total = add_up([final_recv[k, q].astype(F32) for k in range(ranks)])
        leaf_out[:, q, :] = jnp.where(block < sep_blocks, total, known_blocks[q]).astype(BF16)

    drain(rhs_recv.at[pl.ds(0, (group - 1) * rhs_width)], send_sems.at[0])
    drain(fwd_recv.at[pl.ds(0, group - 1)], send_sems.at[1])
    drain(rr_buf.at[pl.ds(0, rows_all - 1)], send_sems.at[2])
    drain(half_send, send_sems.at[3])
    drain(pass_buf.at[pl.ds(0, (rows_all - 1) * n_col)], send_sems.at[4])
    drain(back_recv.at[pl.ds(0, ranks - 1)], send_sems.at[7])
    drain(final_recv.at[pl.ds(0, ranks - 1)], send_sems.at[8])
    conclude(child_w, 0, 0, c)
    conclude(child_w, 0, 1, c)
    conclude(child_w, 0, 2, across)
    conclude(off_w, 1, 0, c)
    conclude(off_w, 1, 1, c)
    conclude(off_w, 1, 2, across)

    @pl.when(x == 0)
    def _():
        drain(known_send.at[pl.ds(0, 2 * rows_all - 1)], send_sems.at[5])
        drain(extra_send.at[pl.ds(0, 2 * rows_all - 1)], send_sems.at[6])
        conclude(root_w, 2, 1, c)
        conclude(root_w, 2, 2, across)

    @pl.when(x == 1)
    def _():
        drain(rr_send, send_sems.at[2])
        drain(pass_send, send_sems.at[4])
        conclude(root_w, 2, 0, c)


def fused(
    rhs_root, rhs_child, subtree_update, inv_root, inv_child, off_child, child_map, subtree_map
):
    n_col = lax.axis_size("col")
    n_row = lax.axis_size("row")
    n_leaf = lax.axis_size("leaf")
    panel = rhs_child.shape[0]
    sep = rhs_child.shape[2]
    ranks = n_row * (n_leaf // 2)
    rows_all = n_leaf * n_row
    group = 2 * ranks
    root_width = inv_root.shape[2]
    child_width = inv_child.shape[2]
    sep_blocks = child_width * n_col // BLOCK_ROWS
    root_blocks = root_width * n_col // BLOCK_ROWS
    piece = n_col * sep
    mixed = n_col + piece // BLOCK_ROWS

    vmem = pl.BlockSpec(memory_space=pltpu.VMEM)
    hbm = pl.BlockSpec(memory_space=pl.ANY)
    buffer = lambda *shape: pltpu.VMEM(shape, BF16)
    return pl.pallas_call(
        solve_kernel,
        out_shape=(
            jax.ShapeDtypeStruct((panel, n_col, sep), F32),
            jax.ShapeDtypeStruct((panel, n_col, sep), F32),
            jax.ShapeDtypeStruct((panel, n_col, BLOCK_ROWS), BF16),
        ),
        in_specs=[hbm] * 8,
        out_specs=(vmem, vmem, vmem),
        scratch_shapes=[
            pltpu.SMEM(child_map.shape, jnp.int32), pltpu.SMEM(subtree_map.shape, jnp.int32),
            buffer(*subtree_update.shape), buffer(*rhs_child.shape), buffer(*rhs_root.shape),
            buffer(n_col, *inv_root.shape), buffer(n_col, *inv_child.shape),
            buffer(n_col, *off_child.shape),
            buffer(2, n_col + 2, panel, BLOCK_ROWS),
            buffer(group * (n_col + 2) + 1, panel, BLOCK_ROWS),
            buffer(n_col, panel, sep), buffer(2 * rows_all, n_col, panel, sep),
            buffer(2, 2, 2 * panel, sep), buffer(group, 2, 2 * panel, sep),
            buffer(n_col + 2, panel, BLOCK_ROWS), buffer(n_col + 2, panel, BLOCK_ROWS),
            pltpu.VMEM((2, n_col, panel, BLOCK_ROWS), F32), buffer(n_col, panel, sep),
            buffer(n_col, panel, BLOCK_ROWS), buffer(2 * rows_all * n_col + 1, panel, BLOCK_ROWS),
            pltpu.VMEM((n_col, 2 * panel, root_width), F32),
            buffer(root_blocks, 2 * panel, BLOCK_ROWS),
            buffer(2 * rows_all, n_col, panel, BLOCK_ROWS),
            buffer(rows_all, n_col, panel, BLOCK_ROWS),
            buffer(2 * rows_all, mixed, panel, BLOCK_ROWS),
            buffer(rows_all, mixed, panel, BLOCK_ROWS),
            buffer(ranks, panel, piece), buffer(ranks, panel, piece),
            buffer(sep_blocks, panel, BLOCK_ROWS),
            buffer(ranks, mixed, panel, BLOCK_ROWS), buffer(ranks, mixed, panel, BLOCK_ROWS),
            pltpu.SemaphoreType.DMA((8,)),
            pltpu.SemaphoreType.DMA((9,)),
            pltpu.SemaphoreType.DMA((9,)),
            pltpu.SemaphoreType.DMA((3, 3, 4)),
            pltpu.SemaphoreType.DMA((3, 3, 4)),
        ],
        compiler_params=pltpu.CompilerParams(
            collective_id=0, has_side_effects=True, vmem_limit_bytes=60 * 1024 * 1024
        ),
    )(
        child_map, subtree_map, subtree_update, rhs_child, rhs_root, inv_root, inv_child, off_child,
    )


def body(*arrays):
    whole_blocks = (
        lax.axis_size("leaf") == 4
        and lax.axis_size("row") == 2
        and lax.axis_size("col") == 4
        and arrays[2].shape[2] == BLOCK_ROWS
        and arrays[4].shape[2] % BLOCK_ROWS == 0
        and arrays[0].shape[0] % 16 == 0
        and arrays[0].shape[2] % 16 == 0
        and arrays[0].shape[2] <= BLOCK_ROWS
        and arrays[0].shape[1] * arrays[0].shape[2] % BLOCK_ROWS == 0
    )
    return (fused if whole_blocks else local)(*arrays)


def solution(mesh):
    in_specs = (
        P("col", None, ("leaf", "row")),
        P("col", None, ("leaf", "row")),
        P("col", None, ("leaf", "row")),
        P(None, ("leaf", "row"), "col"),
        P(None, ("leaf", "row"), "col"),
        P(None, ("leaf", "row"), "col"),
        P(),
        P(),
    )
    out_specs = (
        P("col", None, ("leaf", "row")),
        P("col", None, ("leaf", "row")),
        P("col", None, ("leaf", "row")),
    )
    return jax.shard_map(body, mesh=mesh, in_specs=in_specs, out_specs=out_specs, check_vma=False)
```

```python
import functools

import jax
import jax.numpy as jnp
from jax import lax
from jax.experimental import pallas as pl
from jax.experimental.pallas import tpu as pltpu
from jax.sharding import PartitionSpec as P

BLOCK_ROWS = 128


def partner_2(block, axis, bit):
    count = lax.axis_size(axis)
    route = []
    for low in range(count):
        high = low | 1 << bit
        if high != low and high < count:
            route += [(low, high), (high, low)]
    return lax.ppermute(block, axis, route)


def group_gather(piece, group_size):
    merged = lax.all_gather(piece, "row", axis=2, tiled=True)
    leaf_index = lax.axis_index("leaf")
    for bit_number in range(group_size.bit_length() - 1):
        partner = partner_2(merged, "leaf", bit_number)
        upper = leaf_index >> bit_number & 1 == 1
        merged = jnp.where(
            upper, jnp.concatenate([partner, merged], 2), jnp.concatenate([merged, partner], 2)
        )
    return merged


def group_sum(partial_sum, group_size):
    leaf_index = lax.axis_index("leaf")
    for bit_number in reversed(range(group_size.bit_length() - 1)):
        middle = partial_sum.shape[1] // 2
        lower_half = partial_sum[:, :middle]
        upper_half = partial_sum[:, middle:]
        upper = leaf_index >> bit_number & 1 == 1
        outgoing = jnp.where(upper, lower_half, upper_half)
        kept_half = jnp.where(upper, upper_half, lower_half)
        partial_sum = kept_half + partner_2(
            outgoing.astype(jnp.bfloat16), "leaf", bit_number
        ).astype(outgoing.dtype)
    return lax.psum_scatter(
        partial_sum.astype(jnp.bfloat16), "row", scatter_dimension=1, tiled=True
    ).astype(jnp.float32)


def one_hot(block_map, blocks_total):
    return (block_map[..., None] == jnp.arange(blocks_total, dtype=jnp.int32)).astype(jnp.bfloat16)


def pick_piece(source, position, along):
    return lax.dynamic_index_in_dim(source, position, along, keepdims=False)


def contract(left_side, right_side, left_dim, right_dim):
    return lax.dot_general(
        left_side,
        right_side,
        (((left_dim,), (right_dim,)), ((), ())),
        preferred_element_type=jnp.float32,
    )


def local(
    rhs_root, rhs_child, subtree_update, inv_root, inv_child, off_child, child_map, subtree_map
):
    n_col = lax.axis_size("col")
    n_row = lax.axis_size("row")
    n_leaf = lax.axis_size("leaf")
    group_size = n_leaf // 2
    sub_size = n_leaf // 4
    col_index = lax.axis_index("col")
    leaf_index = lax.axis_index("leaf")
    row_index = lax.axis_index("row")
    front_index = leaf_index // group_size
    member = leaf_index % group_size
    child_rank = member * n_row + row_index
    half_index = member // sub_size
    sub_rank = member % sub_size * n_row + row_index
    panel_width = rhs_child.shape[0]
    right_sides = panel_width * n_col
    sep_piece = rhs_child.shape[2]
    upd_piece = subtree_update.shape[2]
    root_width = inv_root.shape[2]
    child_width = inv_child.shape[2]
    child_order = child_width * n_col
    child_update = upd_piece * n_col * group_size * n_row
    root_blocks = root_width * n_col // BLOCK_ROWS
    child_blocks = (child_order + child_update) // BLOCK_ROWS
    root_matrix = inv_root.reshape(n_col * sep_piece, root_width)
    child_matrix = inv_child.reshape(n_col * sep_piece, child_width)
    off_matrix = off_child.reshape(n_col * upd_piece, child_width)
    joined = jnp.concatenate([subtree_update, rhs_child], 2)
    gathered = group_gather(joined, group_size).reshape(
        panel_width, n_col, group_size * n_row, upd_piece + sep_piece
    )
    sub_vectors = (
        gathered[..., :upd_piece]
        .reshape(panel_width, n_col, 2, -1)
        .transpose(2, 0, 1, 3)
        .reshape(2, panel_width, -1, BLOCK_ROWS)
    )
    child_rhs_full = gathered[..., upd_piece:].reshape(panel_width, child_order)
    sub_rows = lax.dynamic_slice_in_dim(subtree_map, 2 * front_index, 2, 0)
    spread = jnp.einsum(
        "hpjt,hjn->pnt",
        sub_vectors,
        one_hot(sub_rows, child_blocks),
        preferred_element_type=jnp.float32,
    ).reshape(panel_width, -1)
    child_sep = (spread[:, :child_order] + child_rhs_full.astype(jnp.float32)).astype(jnp.bfloat16)
    child_tail = spread[:, child_order:]
    child_tile = lax.all_to_all(
        child_sep.reshape(panel_width, n_col, child_width),
        "col",
        split_axis=1,
        concat_axis=0,
        tiled=True,
    ).reshape(right_sides, child_width)
    child_forward = lax.psum(contract(child_tile, child_matrix, 1, 1), "col").astype(jnp.bfloat16)
    forward_quarter = lax.dynamic_slice_in_dim(
        child_forward.reshape(right_sides, n_col, sep_piece), col_index, 1, 1
    )
    forward_tile = group_gather(forward_quarter, group_size).reshape(right_sides, child_width)
    pass_term = lax.psum_scatter(
        contract(forward_tile, off_matrix, 1, 1), "col", scatter_dimension=0, tiled=True
    )
    tail_mine = pick_piece(
        child_tail.reshape(panel_width, n_col, group_size * n_row, upd_piece), child_rank, 2
    )
    child_pass = (tail_mine - pass_term.reshape(panel_width, n_col, upd_piece)).astype(jnp.bfloat16)
    joined_root = jnp.concatenate([child_pass, rhs_root], 2)
    root_all = lax.all_gather(joined_root, ("leaf", "row"), axis=2, tiled=True).reshape(
        panel_width, n_col, n_leaf * n_row, upd_piece + sep_piece
    )
    pass_vectors = (
        root_all[..., :upd_piece]
        .reshape(panel_width, n_col, 2, -1)
        .transpose(2, 0, 1, 3)
        .reshape(2, panel_width, -1, BLOCK_ROWS)
    )
    root_rhs_full = root_all[..., upd_piece:].reshape(panel_width, root_width * n_col)
    root_spread = jnp.einsum(
        "hpjt,hjn->pnt",
        pass_vectors,
        one_hot(child_map, root_blocks),
        preferred_element_type=jnp.float32,
    ).reshape(panel_width, -1)
    root_sep = (root_spread + root_rhs_full.astype(jnp.float32)).astype(jnp.bfloat16)
    root_tile = lax.all_to_all(
        root_sep.reshape(panel_width, n_col, root_width),
        "col",
        split_axis=1,
        concat_axis=0,
        tiled=True,
    ).reshape(right_sides, root_width)
    root_forward = lax.psum(contract(root_tile, root_matrix, 1, 1), "col").astype(jnp.bfloat16)
    map_row = pick_piece(child_map, front_index, 0)
    root_piece = lax.psum_scatter(
        contract(root_matrix, root_forward, 0, 1), ("leaf", "row"), scatter_dimension=0, tiled=True
    )
    solution_root = lax.all_to_all(
        root_piece.T.reshape(right_sides, 1, sep_piece),
        "col",
        split_axis=0,
        concat_axis=1,
        tiled=True,
    )
    root_everywhere = lax.all_gather(
        solution_root.astype(jnp.bfloat16), ("leaf", "row"), axis=2, tiled=True
    ).reshape(panel_width, root_blocks, BLOCK_ROWS)
    known_full = (
        jnp.einsum(
            "pnt,jn->pjt",
            root_everywhere,
            one_hot(map_row, root_blocks),
            preferred_element_type=jnp.float32,
        )
        .astype(jnp.bfloat16)
        .reshape(panel_width, child_update)
    )
    known_mine = pick_piece(
        known_full.reshape(panel_width, n_col, group_size * n_row, upd_piece), child_rank, 2
    )
    known_rows = lax.all_gather(known_mine, "col", axis=0, tiled=True).reshape(
        right_sides, n_col * upd_piece
    )
    correction = group_sum(contract(known_rows, off_matrix, 1, 0), group_size)
    back_quarter = (
        forward_quarter.reshape(right_sides, sep_piece).astype(jnp.float32) - correction
    ).astype(jnp.bfloat16)
    back_rows = lax.all_gather(
        back_quarter.reshape(right_sides, 1, sep_piece), "col", axis=1, tiled=True
    ).reshape(right_sides, n_col * sep_piece)
    child_piece = group_sum(contract(back_rows, child_matrix, 1, 0), group_size)
    solution_child = lax.all_to_all(
        child_piece.reshape(right_sides, 1, sep_piece),
        "col",
        split_axis=0,
        concat_axis=1,
        tiled=True,
    )
    child_rounded = solution_child.astype(jnp.bfloat16)
    sep_whole = group_gather(child_rounded, group_size).reshape(panel_width, child_order)
    child_whole = jnp.concatenate([sep_whole, known_full], 1)
    sub_row = pick_piece(subtree_map, 2 * front_index + half_index, 0)
    leaf_full = jnp.einsum(
        "pnt,jn->pjt",
        child_whole.reshape(panel_width, child_blocks, BLOCK_ROWS),
        one_hot(sub_row, child_blocks),
        preferred_element_type=jnp.float32,
    ).astype(jnp.bfloat16)
    leaf_solution = pick_piece(
        leaf_full.reshape(panel_width, n_col, sub_size * n_row, upd_piece), sub_rank, 2
    )
    return (solution_root, solution_child, leaf_solution)


F32 = jnp.float32
BF16 = jnp.bfloat16


def add_up(terms):
    total = terms[0]
    for term in terms[1:]:
        total = total + term
    return total


def solve_kernel(
    child_hbm_map, subtree_hbm_map, sub_hbm, rc_hbm, rr_hbm, root_hbm, child_hbm, off_hbm,
    root_out, child_out, leaf_out,
    child_map, subtree_map, sub_in, rc_in, rr_in,
    root_w, child_w, off_w,
    rhs_send, rhs_recv, rr_send, rr_buf,
    fwd_send, fwd_recv, half_send, half_recv, half_own, forward_own,
    pass_send, pass_buf, root_x, solved,
    known_send, known_recv, extra_send, extra_recv,
    whole_send, whole_recv, back_send, back_recv, final_blocks, final_send, final_recv,
    load_sems, send_sems, recv_sems, share_sems, shared_sems,
):
    n_leaf, n_row, n_col = lax.axis_size("leaf"), lax.axis_size("row"), lax.axis_size("col")
    panel = sub_in.shape[0]
    sep = rc_in.shape[2]
    ranks = n_row * (n_leaf // 2)
    rows_all = n_leaf * n_row
    child_tile_blocks = child_w.shape[3] // BLOCK_ROWS
    root_tile_blocks = root_w.shape[3] // BLOCK_ROWS
    sep_blocks = child_tile_blocks * n_col
    piece_blocks = n_col * sep // BLOCK_ROWS
    c = lax.axis_index("col")
    leaf = lax.axis_index("leaf")
    row = lax.axis_index("row")
    x = lax.div(c, 2)
    core = lax.rem(c, 2)
    front = lax.div(leaf, 2)
    low = lax.rem(leaf, 2)
    rank = low * n_row + row
    r = leaf * n_row + row
    pair = 2 * x + 1 - core
    across = 2 * (1 - x) + core
    far = 2 * (1 - x) + 1 - core

    loads = [
        pltpu.make_async_copy(source, target, load_sems.at[number])
        for number, (source, target) in enumerate((
            (sub_hbm, sub_in), (rc_hbm, rc_in),
            (subtree_hbm_map, subtree_map), (child_hbm_map, child_map),
            (child_hbm, child_w.at[c]), (root_hbm, root_w.at[c]),
            (off_hbm, off_w.at[c]), (rr_hbm, rr_in),
        ))
    ]
    for load in loads:
        load.start()

    def flip(m):
        other_leaf = 2 * (1 - front if m & 4 else front) + (1 - low if m & 2 else low)
        other_row = 1 - row if m & 1 else row
        return {"leaf": other_leaf, "row": other_row}, other_leaf * n_row + other_row

    def at(m, c2):
        place, _ = flip(m)
        return {**place, "col": c2}

    def push(source, target, phase, device):
        pltpu.make_async_remote_copy(
            src_ref=source,
            dst_ref=target,
            send_sem=send_sems.at[phase],
            recv_sem=recv_sems.at[phase],
            device_id=device,
            device_id_type=pl.DeviceIdType.MESH,
        ).start()

    def drain(view, sem):
        pltpu.make_async_copy(view, view, sem).wait()

    barrier = pltpu.get_barrier_semaphore()

    def greet(device):
        pl.semaphore_signal(
            barrier, inc=1, device_id=device, device_id_type=pl.DeviceIdType.MESH
        )

    def tiles_of(full, c2, body, tiles=(3, 2, 1, 0)):
        for q in tiles:
            if full:
                body(q)
            else:
                pl.when(q >= c2)(functools.partial(body, q))

    def hand(weights, slot, q, number, kind, c2):
        pltpu.make_async_remote_copy(
            src_ref=weights.at[slot, q],
            dst_ref=weights.at[slot, q],
            send_sem=share_sems.at[number, kind, q],
            recv_sem=shared_sems.at[number, kind, q],
            device_id={"leaf": leaf, "row": row, "col": c2},
            device_id_type=pl.DeviceIdType.MESH,
        ).start()

    def share_across(weights, number, tiles=(3, 2, 1, 0)):
        tiles_of(number == 1, c, lambda q: hand(weights, c, q, number, 0, across), tiles)

    def share_pair(weights, number):
        tiles_of(number < 2, c, lambda q: hand(weights, c, q, number, 1, pair))

    def settle_pair(weights, number):
        tiles_of(number < 2, pair, lambda q: drain(weights.at[0, q], shared_sems.at[number, 1, q]))

    def relay(weights, number):
        def pass_on(q):
            drain(weights.at[across, q], shared_sems.at[number, 0, q])
            hand(weights, across, q, number, 2, pair)

        tiles_of(number == 1, across, pass_on)

    def settle_far(weights, number):
        tiles_of(number == 1, far, lambda q: drain(weights.at[0, q], shared_sems.at[number, 2, q]))

    def conclude(weights, number, kind, slot):
        full = number == 1 or (number == 0 and kind == 1)
        tiles_of(full, slot, lambda q: drain(weights.at[0, q], share_sems.at[number, kind, q]))

    def lower(weights, c2):
        return weights[c2, c2:].reshape(-1, weights.shape[3])

    def flat(weights, c2):
        return weights[c2].reshape(-1, weights.shape[3])

    for m in range(rows_all):
        if m > 0:
            greet(at(m, c))
        greet(at(m, across))
    greet(at(0, pair))

    loads[0].wait()
    loads[1].wait()
    loads[7].wait()
    pad = jnp.zeros((panel, BLOCK_ROWS - sep), BF16)
    for q in range(n_col):
        value = sub_in[:, q, :]
        for half in range(2):
            rhs_send[half, q] = value
        rhs_send[q // 2, n_col + q % 2] = jnp.concatenate([rc_in[:, q, :], pad], 1)
    rr_send[...] = jnp.concatenate([rr_in[:, q, :] for q in range(n_col)], 1)
    rhs_width = rhs_send.shape[1]
    group = 2 * ranks
    no_rhs = group * rhs_width
    no_pass = 2 * rows_all * n_col
    rhs_recv[no_rhs] = jnp.zeros((panel, BLOCK_ROWS), BF16)
    pass_buf[no_pass] = jnp.zeros((panel, BLOCK_ROWS), BF16)
    pl.semaphore_wait(barrier, 2 * rows_all)

    for side in (1, 0):
        for m in reversed(range(ranks)):
            if side or m:
                half = 1 - x if side else x
                push(
                    rhs_send.at[half],
                    rhs_recv.at[pl.ds((x * ranks + rank) * rhs_width, rhs_width)],
                    0,
                    at(m, across if side else c),
                )
    rhs_recv[pl.ds((x * ranks + rank) * rhs_width, rhs_width)] = rhs_send[x]
    loads[4].wait()
    share_pair(child_w, 0)
    loads[5].wait()
    loads[6].wait()
    share_pair(off_w, 1)

    @pl.when(x == 0)
    def _():
        rr_buf[r] = rr_send[...]

    @pl.when(x == 1)
    def _():
        share_across(root_w, 2)

    loads[2].wait()
    loads[3].wait()
    targets = [
        [subtree_map[2 * front + h, j] for j in range(subtree_map.shape[1])] for h in range(2)
    ]

    def sub_place(h, block):
        place = -1
        for j, target in enumerate(targets[h]):
            source = (h * n_row + j % n_row) * rhs_width + j // n_row
            place = jnp.where(target == block, source, place)
        return place

    def sub_value(p, place):
        index = jnp.where(place >= 0, p * ranks * rhs_width + place, no_rhs)
        return rhs_recv[index].astype(F32)

    half_places = [
        [[sub_place(h, (2 * x + i) * child_tile_blocks + b) for h in range(2)]
         for b in range(child_tile_blocks)]
        for i in range(2)
    ]
    drain(rhs_recv.at[pl.ds(0, (group - 1) * rhs_width)], recv_sems.at[0])
    settle_pair(child_w, 0)
    partial_sum = None
    for i in range(2):
        rows = []
        for p in range(2):
            rhs = jnp.concatenate(
                [
                    rhs_recv[(p * ranks + k) * rhs_width + n_col + i][:, :sep].astype(F32)
                    for k in range(ranks)
                ],
                1,
            )
            placed = jnp.concatenate(
                [
                    sub_value(p, half_places[i][b][0]) + sub_value(p, half_places[i][b][1])
                    for b in range(child_tile_blocks)
                ],
                1,
            )
            rows.append(rhs + placed)
        term = contract(
            jnp.concatenate(rows, 0).astype(BF16), flat(child_w, 2 * x + i), 1, 1
        )
        partial_sum = term if partial_sum is None else partial_sum + term
    for q in range(n_col):
        fwd_send[q // 2, q % 2] = partial_sum[:, q * sep : (q + 1) * sep].astype(BF16)

    for side in (1, 0):
        for m in reversed(range(ranks)):
            if side or m:
                half = 1 - x if side else x
                push(
                    fwd_send.at[half], fwd_recv.at[x * ranks + rank], 1,
                    at(m, across if side else c),
                )
    fwd_recv[x * ranks + rank] = fwd_send[x]

    @pl.when(x == 0)
    def _():
        share_pair(root_w, 2)

    @pl.when(x == 1)
    def _():
        pass

    tail = []
    for q in range(n_col):
        block = sep_blocks + q * ranks + rank
        tail.append(sub_value(x, sub_place(0, block)) + sub_value(x, sub_place(1, block)))
    settle_pair(off_w, 1)
    drain(fwd_recv.at[pl.ds(0, group - 1)], recv_sems.at[1])
    z = None
    for i in range(2):
        y = jnp.concatenate(
            [
                fwd_recv[k, i].astype(F32) + fwd_recv[ranks + k, i].astype(F32)
                for k in range(ranks)
            ],
            1,
        ).astype(BF16)
        term = contract(y, flat(off_w, 2 * x + i), 1, 1)
        z = term if z is None else z + term
    for p in range(2):
        for q in range(n_col):
            half_own[p, q] = z[p * panel : (p + 1) * panel, q * BLOCK_ROWS : (q + 1) * BLOCK_ROWS]
    for q in range(n_col):
        half_send[q] = half_own[1 - x, q].astype(BF16)
    for i in range(2):
        mine = (fwd_recv[rank, i].astype(F32) + fwd_recv[ranks + rank, i].astype(F32)).astype(BF16)
        other = jnp.where(x == 0, mine[panel:], mine[:panel])
        half_send[n_col + i] = jnp.concatenate([other, pad], 1)
        forward_own[2 * x + i] = jnp.where(x == 0, mine[:panel], mine[panel:])
    push(half_send, half_recv, 3, at(0, across))
    pl.when(x == 0)(lambda: share_across(off_w, 1))
    for m in reversed(range(rows_all)):
        if m:
            push(rr_send, rr_buf.at[x * rows_all + r], 2, at(m, core))
    pl.when(x == 1)(lambda: push(rr_send, rr_buf.at[rows_all + r], 2, at(0, core)))

    pl.when(x == 0)(lambda: relay(root_w, 2))
    drain(half_recv, recv_sems.at[3])
    for q in range(n_col):
        total = half_own[x, q] + half_recv[q].astype(F32)
        pass_send[q] = (tail[q] - total).astype(BF16)
    for m in reversed(range(rows_all)):
        if m:
            push(pass_send, pass_buf.at[pl.ds((x * rows_all + r) * n_col, n_col)], 4, at(m, core))

    @pl.when(x == 1)
    def _():
        push(pass_send, pass_buf.at[pl.ds((rows_all + r) * n_col, n_col)], 4, at(0, core))
        share_across(off_w, 1)
        share_across(child_w, 0)

    for i in range(2):
        forward_own[2 * (1 - x) + i] = half_recv[n_col + i][:, :sep]

    @pl.when(x == 0)
    def _():
        pass_buf[pl.ds(r * n_col, n_col)] = pass_send[...]
        maps = [[child_map[f, j] for j in range(child_map.shape[1])] for f in range(2)]

        def pass_place(f, block):
            place = -1
            for j, target in enumerate(maps[f]):
                source = (f * ranks + j % ranks) * n_col + j // ranks
                place = jnp.where(target == block, source, place)
            return place

        places = [
            [pass_place(f, block) for f in range(2)] for block in range(root_tile_blocks * n_col)
        ]
        drain(rr_buf.at[pl.ds(0, 2 * rows_all - 1)], recv_sems.at[2])
        for q in range(n_col):
            root_x[q] = jnp.concatenate(
                [
                    jnp.concatenate(
                        [
                            rr_buf[p * rows_all + k][:, q * sep : (q + 1) * sep].astype(F32)
                            for k in range(rows_all)
                        ],
                        1,
                    )
                    for p in range(2)
                ],
                0,
            )
        settle_pair(root_w, 2)
        settle_far(root_w, 2)
        drain(pass_buf.at[pl.ds(0, (2 * rows_all - 1) * n_col)], recv_sems.at[4])

        def pass_value(p, block):
            total = None
            for f in range(2):
                place = places[block][f]
                index = jnp.where(place >= 0, p * rows_all * n_col + place, no_pass)
                value = pass_buf[index].astype(F32)
                total = value if total is None else total + value
            return total

        terms = []
        for c2 in range(n_col):
            passed = jnp.concatenate(
                [
                    jnp.concatenate(
                        [pass_value(p, c2 * root_tile_blocks + b) for b in range(root_tile_blocks)],
                        1,
                    )
                    for p in range(2)
                ],
                0,
            )
            term = contract((root_x[c2] + passed).astype(BF16), lower(root_w, c2), 1, 1)
            if c2 > 0:
                term = jnp.concatenate([jnp.zeros((2 * panel, c2 * sep), F32), term], 1)
            terms.append(term)
        root_forward = add_up(terms)
        totals = []
        for c2 in range(n_col):
            total = contract(
                root_forward[:, c2 * sep :].astype(BF16), lower(root_w, c2), 1, 0
            )
            for b in range(root_tile_blocks):
                solved[c2 * root_tile_blocks + b] = total[
                    :, b * BLOCK_ROWS : (b + 1) * BLOCK_ROWS
                ].astype(BF16)
            totals.append(total)
        for r2 in range(rows_all):
            for q in range(n_col):
                block = solved[child_map[r2 // ranks, q * ranks + r2 % ranks]]
                for p in range(2):
                    known_send[2 * r2 + p, q] = block[p * panel : (p + 1) * panel]
        for m in reversed(range(rows_all)):
            _, r2 = flip(m)
            push(known_send.at[2 * r2 + 1], known_recv.at[r], 5, at(m, across))
            if m:
                push(known_send.at[2 * r2], known_recv.at[r], 5, at(m, c))
        share_across(child_w, 0)
        known_recv[r] = known_send[2 * r]
        for r2 in range(rows_all):
            piece = jnp.concatenate(
                [total[:, r2 * sep : (r2 + 1) * sep] for total in totals], 1
            ).astype(BF16)
            for p in range(2):
                for b in range(piece_blocks):
                    extra_send[2 * r2 + p, b] = piece[
                        p * panel : (p + 1) * panel, b * BLOCK_ROWS : (b + 1) * BLOCK_ROWS
                    ]
        for m in reversed(range(rows_all)):
            _, r2 = flip(m)
            push(extra_send.at[2 * r2 + 1], extra_recv.at[r], 6, at(m, across))
            if m:
                push(extra_send.at[2 * r2], extra_recv.at[r], 6, at(m, c))
        extra_recv[r] = extra_send[2 * r]

    relay(off_w, 1)
    settle_far(off_w, 1)

    def from_root(buffer, phase):
        pl.when(x == 0)(lambda: drain(buffer.at[pl.ds(0, rows_all - 1)], recv_sems.at[phase]))
        pl.when(x == 1)(lambda: drain(buffer, recv_sems.at[phase]))

    from_root(known_recv, 5)
    known = jnp.concatenate(
        [
            add_up([known_recv[k, q].astype(F32) for k in range(rows_all)])
            for q in range(n_col)
        ],
        1,
    ).astype(BF16)
    corrections = [contract(known, flat(off_w, c2), 1, 0) for c2 in range(n_col)]
    for k in range(ranks):
        back_send[k] = jnp.concatenate(
            [term[:, k * sep : (k + 1) * sep] for term in corrections], 1
        ).astype(BF16)

    def rank_of(m):
        _, r2 = flip(m)
        return r2 - front * ranks

    for m in reversed(range(1, ranks)):
        push(back_send.at[rank_of(m)], back_recv.at[rank], 7, at(m, c))
    back_recv[rank] = back_send[rank]
    for q in range(n_col):
        whole_send[q] = known[:, q * BLOCK_ROWS : (q + 1) * BLOCK_ROWS]
    for m in reversed(range(1, ranks)):
        push(whole_send, whole_recv.at[pl.ds(rank * n_col, n_col)], 9, at(m, c))
    whole_recv[pl.ds(rank * n_col, n_col)] = whole_send[...]
    relay(child_w, 0)
    own = jnp.concatenate([forward_own[q].astype(F32) for q in range(n_col)], 1)
    settle_far(child_w, 0)
    drain(back_recv.at[pl.ds(0, ranks - 1)], recv_sems.at[7])
    back = own - add_up([back_recv[k].astype(F32) for k in range(ranks)])
    totals = []
    for c2 in range(n_col):
        total = contract(back[:, c2 * sep :].astype(BF16), lower(child_w, c2), 1, 0)
        for b in range(child_tile_blocks):
            final_blocks[c2 * child_tile_blocks + b] = total[
                :, b * BLOCK_ROWS : (b + 1) * BLOCK_ROWS
            ].astype(BF16)
        totals.append(total)
    for k in range(ranks):
        for q in range(n_col):
            block = subtree_map[2 * front + k // n_row, q * n_row + k % n_row]
            final_send[k, q] = final_blocks[jnp.minimum(block, sep_blocks - 1)]
        piece = jnp.concatenate(
            [total[:, k * sep : (k + 1) * sep] for total in totals], 1
        ).astype(BF16)
        for b in range(piece_blocks):
            final_send[k, n_col + b] = piece[:, b * BLOCK_ROWS : (b + 1) * BLOCK_ROWS]
    for m in reversed(range(1, ranks)):
        push(final_send.at[rank_of(m)], final_recv.at[rank], 8, at(m, c))
    final_recv[rank] = final_send[rank]

    def piece_of(buffer, count, first):
        total = jnp.concatenate(
            [
                add_up([buffer[k, first + b].astype(F32) for k in range(count)])
                for b in range(piece_blocks)
            ],
            1,
        )
        return total.reshape(panel, n_col, sep)

    from_root(extra_recv, 6)
    root_out[...] = piece_of(extra_recv, rows_all, 0)
    drain(whole_recv.at[pl.ds(0, (ranks - 1) * n_col)], recv_sems.at[9])
    drain(final_recv.at[pl.ds(0, ranks - 1)], recv_sems.at[8])
    child_out[...] = piece_of(final_recv, ranks, n_col)
    for q in range(n_col):
        block = subtree_map[leaf, q * n_row + row]
        total = add_up([final_recv[k, q].astype(F32) for k in range(ranks)])
        j = jnp.maximum(block - sep_blocks, 0)
        whole = whole_recv[lax.rem(j, ranks) * n_col + lax.div(j, ranks)]
        leaf_out[:, q, :] = jnp.where(block < sep_blocks, total.astype(BF16), whole)

    drain(rhs_recv.at[pl.ds(0, (group - 1) * rhs_width)], send_sems.at[0])
    drain(fwd_recv.at[pl.ds(0, group - 1)], send_sems.at[1])
    drain(rr_buf.at[pl.ds(0, rows_all - 1)], send_sems.at[2])
    drain(half_send, send_sems.at[3])
    drain(pass_buf.at[pl.ds(0, (rows_all - 1) * n_col)], send_sems.at[4])
    drain(back_recv.at[pl.ds(0, ranks - 1)], send_sems.at[7])
    drain(final_recv.at[pl.ds(0, ranks - 1)], send_sems.at[8])
    drain(whole_recv.at[pl.ds(0, (ranks - 1) * n_col)], send_sems.at[9])
    conclude(child_w, 0, 0, c)
    conclude(child_w, 0, 1, c)
    conclude(child_w, 0, 2, across)
    conclude(off_w, 1, 0, c)
    conclude(off_w, 1, 1, c)
    conclude(off_w, 1, 2, across)

    @pl.when(x == 0)
    def _():
        drain(known_send.at[pl.ds(0, 2 * rows_all - 1)], send_sems.at[5])
        drain(extra_send.at[pl.ds(0, 2 * rows_all - 1)], send_sems.at[6])
        conclude(root_w, 2, 1, c)
        conclude(root_w, 2, 2, across)

    @pl.when(x == 1)
    def _():
        drain(rr_send, send_sems.at[2])
        drain(pass_send, send_sems.at[4])
        conclude(root_w, 2, 0, c)


def place_kernel(*refs):
    copies = [
        pltpu.make_async_copy(refs[k], refs[3 + k], refs[6].at[k]) for k in range(3)
    ]
    for copy in copies:
        copy.start()
    for copy in copies:
        copy.wait()


def fused(
    rhs_root, rhs_child, subtree_update, inv_root, inv_child, off_child, child_map, subtree_map
):
    n_col = lax.axis_size("col")
    n_row = lax.axis_size("row")
    n_leaf = lax.axis_size("leaf")
    panel = rhs_child.shape[0]
    sep = rhs_child.shape[2]
    ranks = n_row * (n_leaf // 2)
    rows_all = n_leaf * n_row
    group = 2 * ranks
    root_width = inv_root.shape[2]
    child_width = inv_child.shape[2]
    sep_blocks = child_width * n_col // BLOCK_ROWS
    root_blocks = root_width * n_col // BLOCK_ROWS
    piece = n_col * sep
    mixed = n_col + piece // BLOCK_ROWS

    vmem = pl.BlockSpec(memory_space=pltpu.VMEM)
    hbm = pl.BlockSpec(memory_space=pl.ANY)
    buffer = lambda *shape: pltpu.VMEM(shape, BF16)
    outs = pl.pallas_call(
        solve_kernel,
        out_shape=(
            jax.ShapeDtypeStruct((panel, n_col, sep), F32),
            jax.ShapeDtypeStruct((panel, n_col, sep), F32),
            jax.ShapeDtypeStruct((panel, n_col, BLOCK_ROWS), BF16),
        ),
        in_specs=[hbm] * 8,
        out_specs=(vmem, vmem, vmem),
        scratch_shapes=[
            pltpu.SMEM(child_map.shape, jnp.int32), pltpu.SMEM(subtree_map.shape, jnp.int32),
            buffer(*subtree_update.shape), buffer(*rhs_child.shape), buffer(*rhs_root.shape),
            buffer(n_col, *inv_root.shape), buffer(n_col, *inv_child.shape),
            buffer(n_col, *off_child.shape),
            buffer(2, n_col + 2, panel, BLOCK_ROWS),
            buffer(group * (n_col + 2) + 1, panel, BLOCK_ROWS),
            buffer(panel, piece), buffer(2 * rows_all, panel, piece),
            buffer(2, 2, 2 * panel, sep), buffer(group, 2, 2 * panel, sep),
            buffer(n_col + 2, panel, BLOCK_ROWS), buffer(n_col + 2, panel, BLOCK_ROWS),
            pltpu.VMEM((2, n_col, panel, BLOCK_ROWS), F32), buffer(n_col, panel, sep),
            buffer(n_col, panel, BLOCK_ROWS), buffer(2 * rows_all * n_col + 1, panel, BLOCK_ROWS),
            pltpu.VMEM((n_col, 2 * panel, root_width), F32),
            buffer(root_blocks, 2 * panel, BLOCK_ROWS),
            buffer(2 * rows_all, n_col, panel, BLOCK_ROWS),
            buffer(rows_all, n_col, panel, BLOCK_ROWS),
            buffer(2 * rows_all, piece // BLOCK_ROWS, panel, BLOCK_ROWS),
            buffer(rows_all, piece // BLOCK_ROWS, panel, BLOCK_ROWS),
            buffer(n_col, panel, BLOCK_ROWS), buffer(ranks * n_col, panel, BLOCK_ROWS),
            buffer(ranks, panel, piece), buffer(ranks, panel, piece),
            buffer(sep_blocks, panel, BLOCK_ROWS),
            buffer(ranks, mixed, panel, BLOCK_ROWS), buffer(ranks, mixed, panel, BLOCK_ROWS),
            pltpu.SemaphoreType.DMA((8,)),
            pltpu.SemaphoreType.DMA((10,)),
            pltpu.SemaphoreType.DMA((10,)),
            pltpu.SemaphoreType.DMA((3, 3, 4)),
            pltpu.SemaphoreType.DMA((3, 3, 4)),
        ],
        compiler_params=pltpu.CompilerParams(
            collective_id=0, has_side_effects=True, vmem_limit_bytes=60 * 1024 * 1024
        ),
    )(
        child_map, subtree_map, subtree_update, rhs_child, rhs_root, inv_root, inv_child, off_child,
    )
    return pl.pallas_call(
        place_kernel,
        out_shape=tuple(jax.ShapeDtypeStruct(out.shape, out.dtype) for out in outs),
        in_specs=[vmem] * 3,
        out_specs=(hbm,) * 3,
        scratch_shapes=[pltpu.SemaphoreType.DMA((3,))],
    )(*outs)


def body(*arrays):
    whole_blocks = (
        lax.axis_size("leaf") == 4
        and lax.axis_size("row") == 2
        and lax.axis_size("col") == 4
        and arrays[2].shape[2] == BLOCK_ROWS
        and arrays[4].shape[2] % BLOCK_ROWS == 0
        and arrays[0].shape[0] % 16 == 0
        and arrays[0].shape[2] % 16 == 0
        and arrays[0].shape[2] <= BLOCK_ROWS
        and arrays[0].shape[1] * arrays[0].shape[2] % BLOCK_ROWS == 0
    )
    return (fused if whole_blocks else local)(*arrays)


def solution(mesh):
    in_specs = (
        P("col", None, ("leaf", "row")),
        P("col", None, ("leaf", "row")),
        P("col", None, ("leaf", "row")),
        P(None, ("leaf", "row"), "col"),
        P(None, ("leaf", "row"), "col"),
        P(None, ("leaf", "row"), "col"),
        P(),
        P(),
    )
    out_specs = (
        P("col", None, ("leaf", "row")),
        P("col", None, ("leaf", "row")),
        P("col", None, ("leaf", "row")),
    )
    return jax.shard_map(body, mesh=mesh, in_specs=in_specs, out_specs=out_specs, check_vma=False)
```

```python
import functools

import jax
import jax.numpy as jnp
from jax import lax
from jax.experimental import pallas as pl
from jax.experimental.pallas import tpu as pltpu
from jax.sharding import PartitionSpec as P

BLOCK_ROWS = 128


def partner_2(block, axis, bit):
    count = lax.axis_size(axis)
    route = []
    for low in range(count):
        high = low | 1 << bit
        if high != low and high < count:
            route += [(low, high), (high, low)]
    return lax.ppermute(block, axis, route)


def group_gather(piece, group_size):
    merged = lax.all_gather(piece, "row", axis=2, tiled=True)
    leaf_index = lax.axis_index("leaf")
    for bit_number in range(group_size.bit_length() - 1):
        partner = partner_2(merged, "leaf", bit_number)
        upper = leaf_index >> bit_number & 1 == 1
        merged = jnp.where(
            upper, jnp.concatenate([partner, merged], 2), jnp.concatenate([merged, partner], 2)
        )
    return merged


def group_sum(partial_sum, group_size):
    leaf_index = lax.axis_index("leaf")
    for bit_number in reversed(range(group_size.bit_length() - 1)):
        middle = partial_sum.shape[1] // 2
        lower_half = partial_sum[:, :middle]
        upper_half = partial_sum[:, middle:]
        upper = leaf_index >> bit_number & 1 == 1
        outgoing = jnp.where(upper, lower_half, upper_half)
        kept_half = jnp.where(upper, upper_half, lower_half)
        partial_sum = kept_half + partner_2(
            outgoing.astype(jnp.bfloat16), "leaf", bit_number
        ).astype(outgoing.dtype)
    return lax.psum_scatter(
        partial_sum.astype(jnp.bfloat16), "row", scatter_dimension=1, tiled=True
    ).astype(jnp.float32)


def one_hot(block_map, blocks_total):
    return (block_map[..., None] == jnp.arange(blocks_total, dtype=jnp.int32)).astype(jnp.bfloat16)


def pick_piece(source, position, along):
    return lax.dynamic_index_in_dim(source, position, along, keepdims=False)


def contract(left_side, right_side, left_dim, right_dim):
    return lax.dot_general(
        left_side,
        right_side,
        (((left_dim,), (right_dim,)), ((), ())),
        preferred_element_type=jnp.float32,
    )


def local(
    rhs_root, rhs_child, subtree_update, inv_root, inv_child, off_child, child_map, subtree_map
):
    n_col = lax.axis_size("col")
    n_row = lax.axis_size("row")
    n_leaf = lax.axis_size("leaf")
    group_size = n_leaf // 2
    sub_size = n_leaf // 4
    col_index = lax.axis_index("col")
    leaf_index = lax.axis_index("leaf")
    row_index = lax.axis_index("row")
    front_index = leaf_index // group_size
    member = leaf_index % group_size
    child_rank = member * n_row + row_index
    half_index = member // sub_size
    sub_rank = member % sub_size * n_row + row_index
    panel_width = rhs_child.shape[0]
    right_sides = panel_width * n_col
    sep_piece = rhs_child.shape[2]
    upd_piece = subtree_update.shape[2]
    root_width = inv_root.shape[2]
    child_width = inv_child.shape[2]
    child_order = child_width * n_col
    child_update = upd_piece * n_col * group_size * n_row
    root_blocks = root_width * n_col // BLOCK_ROWS
    child_blocks = (child_order + child_update) // BLOCK_ROWS
    root_matrix = inv_root.reshape(n_col * sep_piece, root_width)
    child_matrix = inv_child.reshape(n_col * sep_piece, child_width)
    off_matrix = off_child.reshape(n_col * upd_piece, child_width)
    joined = jnp.concatenate([subtree_update, rhs_child], 2)
    gathered = group_gather(joined, group_size).reshape(
        panel_width, n_col, group_size * n_row, upd_piece + sep_piece
    )
    sub_vectors = (
        gathered[..., :upd_piece]
        .reshape(panel_width, n_col, 2, -1)
        .transpose(2, 0, 1, 3)
        .reshape(2, panel_width, -1, BLOCK_ROWS)
    )
    child_rhs_full = gathered[..., upd_piece:].reshape(panel_width, child_order)
    sub_rows = lax.dynamic_slice_in_dim(subtree_map, 2 * front_index, 2, 0)
    spread = jnp.einsum(
        "hpjt,hjn->pnt",
        sub_vectors,
        one_hot(sub_rows, child_blocks),
        preferred_element_type=jnp.float32,
    ).reshape(panel_width, -1)
    child_sep = (spread[:, :child_order] + child_rhs_full.astype(jnp.float32)).astype(jnp.bfloat16)
    child_tail = spread[:, child_order:]
    child_tile = lax.all_to_all(
        child_sep.reshape(panel_width, n_col, child_width),
        "col",
        split_axis=1,
        concat_axis=0,
        tiled=True,
    ).reshape(right_sides, child_width)
    child_forward = lax.psum(contract(child_tile, child_matrix, 1, 1), "col").astype(jnp.bfloat16)
    forward_quarter = lax.dynamic_slice_in_dim(
        child_forward.reshape(right_sides, n_col, sep_piece), col_index, 1, 1
    )
    forward_tile = group_gather(forward_quarter, group_size).reshape(right_sides, child_width)
    pass_term = lax.psum_scatter(
        contract(forward_tile, off_matrix, 1, 1), "col", scatter_dimension=0, tiled=True
    )
    tail_mine = pick_piece(
        child_tail.reshape(panel_width, n_col, group_size * n_row, upd_piece), child_rank, 2
    )
    child_pass = (tail_mine - pass_term.reshape(panel_width, n_col, upd_piece)).astype(jnp.bfloat16)
    joined_root = jnp.concatenate([child_pass, rhs_root], 2)
    root_all = lax.all_gather(joined_root, ("leaf", "row"), axis=2, tiled=True).reshape(
        panel_width, n_col, n_leaf * n_row, upd_piece + sep_piece
    )
    pass_vectors = (
        root_all[..., :upd_piece]
        .reshape(panel_width, n_col, 2, -1)
        .transpose(2, 0, 1, 3)
        .reshape(2, panel_width, -1, BLOCK_ROWS)
    )
    root_rhs_full = root_all[..., upd_piece:].reshape(panel_width, root_width * n_col)
    root_spread = jnp.einsum(
        "hpjt,hjn->pnt",
        pass_vectors,
        one_hot(child_map, root_blocks),
        preferred_element_type=jnp.float32,
    ).reshape(panel_width, -1)
    root_sep = (root_spread + root_rhs_full.astype(jnp.float32)).astype(jnp.bfloat16)
    root_tile = lax.all_to_all(
        root_sep.reshape(panel_width, n_col, root_width),
        "col",
        split_axis=1,
        concat_axis=0,
        tiled=True,
    ).reshape(right_sides, root_width)
    root_forward = lax.psum(contract(root_tile, root_matrix, 1, 1), "col").astype(jnp.bfloat16)
    map_row = pick_piece(child_map, front_index, 0)
    root_piece = lax.psum_scatter(
        contract(root_matrix, root_forward, 0, 1), ("leaf", "row"), scatter_dimension=0, tiled=True
    )
    solution_root = lax.all_to_all(
        root_piece.T.reshape(right_sides, 1, sep_piece),
        "col",
        split_axis=0,
        concat_axis=1,
        tiled=True,
    )
    root_everywhere = lax.all_gather(
        solution_root.astype(jnp.bfloat16), ("leaf", "row"), axis=2, tiled=True
    ).reshape(panel_width, root_blocks, BLOCK_ROWS)
    known_full = (
        jnp.einsum(
            "pnt,jn->pjt",
            root_everywhere,
            one_hot(map_row, root_blocks),
            preferred_element_type=jnp.float32,
        )
        .astype(jnp.bfloat16)
        .reshape(panel_width, child_update)
    )
    known_mine = pick_piece(
        known_full.reshape(panel_width, n_col, group_size * n_row, upd_piece), child_rank, 2
    )
    known_rows = lax.all_gather(known_mine, "col", axis=0, tiled=True).reshape(
        right_sides, n_col * upd_piece
    )
    correction = group_sum(contract(known_rows, off_matrix, 1, 0), group_size)
    back_quarter = (
        forward_quarter.reshape(right_sides, sep_piece).astype(jnp.float32) - correction
    ).astype(jnp.bfloat16)
    back_rows = lax.all_gather(
        back_quarter.reshape(right_sides, 1, sep_piece), "col", axis=1, tiled=True
    ).reshape(right_sides, n_col * sep_piece)
    child_piece = group_sum(contract(back_rows, child_matrix, 1, 0), group_size)
    solution_child = lax.all_to_all(
        child_piece.reshape(right_sides, 1, sep_piece),
        "col",
        split_axis=0,
        concat_axis=1,
        tiled=True,
    )
    child_rounded = solution_child.astype(jnp.bfloat16)
    sep_whole = group_gather(child_rounded, group_size).reshape(panel_width, child_order)
    child_whole = jnp.concatenate([sep_whole, known_full], 1)
    sub_row = pick_piece(subtree_map, 2 * front_index + half_index, 0)
    leaf_full = jnp.einsum(
        "pnt,jn->pjt",
        child_whole.reshape(panel_width, child_blocks, BLOCK_ROWS),
        one_hot(sub_row, child_blocks),
        preferred_element_type=jnp.float32,
    ).astype(jnp.bfloat16)
    leaf_solution = pick_piece(
        leaf_full.reshape(panel_width, n_col, sub_size * n_row, upd_piece), sub_rank, 2
    )
    return (solution_root, solution_child, leaf_solution)


F32 = jnp.float32
BF16 = jnp.bfloat16


def add_up(terms):
    total = terms[0]
    for term in terms[1:]:
        total = total + term
    return total


def solve_kernel(
    child_hbm_map, subtree_hbm_map, sub_hbm, rc_hbm, rr_hbm, root_hbm, child_hbm, off_hbm,
    root_out, child_out, leaf_out,
    child_map, subtree_map, sub_in, rc_in, rr_in,
    root_w, child_w, off_w,
    rhs_send, rhs_recv, rr_send, rr_buf,
    fwd_send, fwd_recv, half_send, half_recv, half_own, forward_own,
    pass_send, pass_buf, root_x, solved,
    known_send, known_recv, extra_send, extra_recv,
    whole_send, whole_recv, back_send, back_recv, final_blocks, final_send, final_recv,
    load_sems, send_sems, recv_sems, share_sems, shared_sems,
):
    n_leaf, n_row, n_col = lax.axis_size("leaf"), lax.axis_size("row"), lax.axis_size("col")
    panel = sub_in.shape[0]
    sep = rc_in.shape[2]
    ranks = n_row * (n_leaf // 2)
    rows_all = n_leaf * n_row
    child_tile_blocks = child_w.shape[3] // BLOCK_ROWS
    root_tile_blocks = root_w.shape[3] // BLOCK_ROWS
    sep_blocks = child_tile_blocks * n_col
    piece_blocks = n_col * sep // BLOCK_ROWS
    c = lax.axis_index("col")
    leaf = lax.axis_index("leaf")
    row = lax.axis_index("row")
    x = lax.div(c, 2)
    core = lax.rem(c, 2)
    front = lax.div(leaf, 2)
    low = lax.rem(leaf, 2)
    rank = low * n_row + row
    r = leaf * n_row + row
    pair = 2 * x + 1 - core
    across = 2 * (1 - x) + core
    far = 2 * (1 - x) + 1 - core

    loads = [
        pltpu.make_async_copy(source, target, load_sems.at[number])
        for number, (source, target) in enumerate((
            (sub_hbm, sub_in), (rc_hbm, rc_in),
            (subtree_hbm_map, subtree_map), (child_hbm_map, child_map),
            (child_hbm, child_w.at[c]), (root_hbm, root_w.at[c]),
            (off_hbm, off_w.at[c]), (rr_hbm, rr_in),
        ))
    ]
    for load in loads:
        load.start()

    def flip(m):
        other_leaf = 2 * (1 - front if m & 4 else front) + (1 - low if m & 2 else low)
        other_row = 1 - row if m & 1 else row
        return {"leaf": other_leaf, "row": other_row}, other_leaf * n_row + other_row

    def at(m, c2):
        place, _ = flip(m)
        return {**place, "col": c2}

    def push(source, target, phase, device):
        pltpu.make_async_remote_copy(
            src_ref=source,
            dst_ref=target,
            send_sem=send_sems.at[phase],
            recv_sem=recv_sems.at[phase],
            device_id=device,
            device_id_type=pl.DeviceIdType.MESH,
        ).start()

    def drain(view, sem):
        pltpu.make_async_copy(view, view, sem).wait()

    barrier = pltpu.get_barrier_semaphore()

    def greet(device):
        pl.semaphore_signal(
            barrier, inc=1, device_id=device, device_id_type=pl.DeviceIdType.MESH
        )

    def tiles_of(full, c2, body, tiles=(3, 2, 1, 0)):
        for q in tiles:
            if full:
                body(q)
            else:
                pl.when(q >= c2)(functools.partial(body, q))

    def hand(weights, slot, q, number, kind, c2):
        pltpu.make_async_remote_copy(
            src_ref=weights.at[slot, q],
            dst_ref=weights.at[slot, q],
            send_sem=share_sems.at[number, kind, q],
            recv_sem=shared_sems.at[number, kind, q],
            device_id={"leaf": leaf, "row": row, "col": c2},
            device_id_type=pl.DeviceIdType.MESH,
        ).start()

    def share_across(weights, number, tiles=(3, 2, 1, 0)):
        tiles_of(number == 1, c, lambda q: hand(weights, c, q, number, 0, across), tiles)

    def share_pair(weights, number):
        tiles_of(number < 2, c, lambda q: hand(weights, c, q, number, 1, pair))

    def settle_pair(weights, number):
        tiles_of(number < 2, pair, lambda q: drain(weights.at[0, q], shared_sems.at[number, 1, q]))

    def relay(weights, number):
        def pass_on(q):
            drain(weights.at[across, q], shared_sems.at[number, 0, q])
            hand(weights, across, q, number, 2, pair)

        tiles_of(number == 1, across, pass_on)

    def settle_far(weights, number):
        tiles_of(number == 1, far, lambda q: drain(weights.at[0, q], shared_sems.at[number, 2, q]))

    def conclude(weights, number, kind, slot):
        full = number == 1 or (number == 0 and kind == 1)
        tiles_of(full, slot, lambda q: drain(weights.at[0, q], share_sems.at[number, kind, q]))

    def lower(weights, c2):
        return weights[c2, c2:].reshape(-1, weights.shape[3])

    def flat(weights, c2):
        return weights[c2].reshape(-1, weights.shape[3])

    for m in range(rows_all):
        if m > 0:
            greet(at(m, c))
        greet(at(m, across))
    greet(at(0, pair))

    loads[0].wait()
    loads[1].wait()
    loads[7].wait()
    pad = jnp.zeros((panel, BLOCK_ROWS - sep), BF16)
    for q in range(n_col):
        value = sub_in[:, q, :]
        for half in range(2):
            rhs_send[half, q] = value
        rhs_send[q // 2, n_col + q % 2] = jnp.concatenate([rc_in[:, q, :], pad], 1)
    rr_send[...] = jnp.concatenate([rr_in[:, q, :] for q in range(n_col)], 1)
    rhs_width = rhs_send.shape[1]
    group = 2 * ranks
    no_rhs = group * rhs_width
    no_pass = 2 * rows_all * n_col
    rhs_recv[no_rhs] = jnp.zeros((panel, BLOCK_ROWS), BF16)
    pass_buf[no_pass] = jnp.zeros((panel, BLOCK_ROWS), BF16)
    pl.semaphore_wait(barrier, 2 * rows_all)

    for side in (1, 0):
        for m in reversed(range(ranks)):
            if side or m:
                half = 1 - x if side else x
                push(
                    rhs_send.at[half],
                    rhs_recv.at[pl.ds((x * ranks + rank) * rhs_width, rhs_width)],
                    0,
                    at(m, across if side else c),
                )
    rhs_recv[pl.ds((x * ranks + rank) * rhs_width, rhs_width)] = rhs_send[x]
    loads[4].wait()
    share_pair(child_w, 0)
    loads[5].wait()
    loads[6].wait()
    share_pair(off_w, 1)

    @pl.when(x == 0)
    def _():
        rr_buf[r] = rr_send[...]

    @pl.when(x == 1)
    def _():
        share_across(root_w, 2)

    loads[2].wait()
    loads[3].wait()
    targets = [
        [subtree_map[2 * front + h, j] for j in range(subtree_map.shape[1])] for h in range(2)
    ]

    def sub_place(h, block):
        place = -1
        for j, target in enumerate(targets[h]):
            source = (h * n_row + j % n_row) * rhs_width + j // n_row
            place = jnp.where(target == block, source, place)
        return place

    def sub_value(p, place):
        index = jnp.where(place >= 0, p * ranks * rhs_width + place, no_rhs)
        return rhs_recv[index].astype(F32)

    half_places = [
        [[sub_place(h, (2 * x + i) * child_tile_blocks + b) for h in range(2)]
         for b in range(child_tile_blocks)]
        for i in range(2)
    ]
    drain(rhs_recv.at[pl.ds(0, (group - 1) * rhs_width)], recv_sems.at[0])
    settle_pair(child_w, 0)
    partial_sum = None
    for i in range(2):
        rows = []
        for p in range(2):
            rhs = jnp.concatenate(
                [
                    rhs_recv[(p * ranks + k) * rhs_width + n_col + i][:, :sep].astype(F32)
                    for k in range(ranks)
                ],
                1,
            )
            placed = jnp.concatenate(
                [
                    sub_value(p, half_places[i][b][0]) + sub_value(p, half_places[i][b][1])
                    for b in range(child_tile_blocks)
                ],
                1,
            )
            rows.append(rhs + placed)
        term = contract(
            jnp.concatenate(rows, 0).astype(BF16), flat(child_w, 2 * x + i), 1, 1
        )
        partial_sum = term if partial_sum is None else partial_sum + term
    for q in range(n_col):
        fwd_send[q // 2, q % 2] = partial_sum[:, q * sep : (q + 1) * sep].astype(BF16)

    for side in (1, 0):
        for m in reversed(range(ranks)):
            if side or m:
                half = 1 - x if side else x
                push(
                    fwd_send.at[half], fwd_recv.at[x * ranks + rank], 1,
                    at(m, across if side else c),
                )
    fwd_recv[x * ranks + rank] = fwd_send[x]

    @pl.when(x == 0)
    def _():
        share_pair(root_w, 2)

    @pl.when(x == 1)
    def _():
        pass

    tail = []
    for q in range(n_col):
        block = sep_blocks + q * ranks + rank
        tail.append(sub_value(x, sub_place(0, block)) + sub_value(x, sub_place(1, block)))
    settle_pair(off_w, 1)
    drain(fwd_recv.at[pl.ds(0, group - 1)], recv_sems.at[1])
    z = None
    for i in range(2):
        y = jnp.concatenate(
            [
                fwd_recv[k, i].astype(F32) + fwd_recv[ranks + k, i].astype(F32)
                for k in range(ranks)
            ],
            1,
        ).astype(BF16)
        term = contract(y, flat(off_w, 2 * x + i), 1, 1)
        z = term if z is None else z + term
    for p in range(2):
        for q in range(n_col):
            half_own[p, q] = z[p * panel : (p + 1) * panel, q * BLOCK_ROWS : (q + 1) * BLOCK_ROWS]
    for q in range(n_col):
        half_send[q] = half_own[1 - x, q].astype(BF16)
    for i in range(2):
        mine = (fwd_recv[rank, i].astype(F32) + fwd_recv[ranks + rank, i].astype(F32)).astype(BF16)
        other = jnp.where(x == 0, mine[panel:], mine[:panel])
        half_send[n_col + i] = jnp.concatenate([other, pad], 1)
        forward_own[2 * x + i] = jnp.where(x == 0, mine[:panel], mine[panel:])
    push(half_send, half_recv, 3, at(0, across))
    pl.when(x == 0)(lambda: share_across(off_w, 1))
    for m in reversed(range(rows_all)):
        if m:
            push(rr_send, rr_buf.at[x * rows_all + r], 2, at(m, core))
    pl.when(x == 1)(lambda: push(rr_send, rr_buf.at[rows_all + r], 2, at(0, core)))

    drain(half_recv, recv_sems.at[3])
    pl.when(x == 0)(lambda: relay(root_w, 2))
    for q in range(n_col):
        total = half_own[x, q] + half_recv[q].astype(F32)
        pass_send[q] = (tail[q] - total).astype(BF16)
    for m in reversed(range(rows_all)):
        if m:
            push(pass_send, pass_buf.at[pl.ds((x * rows_all + r) * n_col, n_col)], 4, at(m, core))

    @pl.when(x == 1)
    def _():
        push(pass_send, pass_buf.at[pl.ds((rows_all + r) * n_col, n_col)], 4, at(0, core))
        drain(pass_buf.at[pl.ds(0, rows_all * n_col)], send_sems.at[4])
        share_across(off_w, 1)
        share_across(child_w, 0)

    for i in range(2):
        forward_own[2 * (1 - x) + i] = half_recv[n_col + i][:, :sep]

    @pl.when(x == 0)
    def _():
        pass_buf[pl.ds(r * n_col, n_col)] = pass_send[...]
        maps = [[child_map[f, j] for j in range(child_map.shape[1])] for f in range(2)]

        def pass_place(f, block):
            place = -1
            for j, target in enumerate(maps[f]):
                source = (f * ranks + j % ranks) * n_col + j // ranks
                place = jnp.where(target == block, source, place)
            return place

        places = [
            [pass_place(f, block) for f in range(2)] for block in range(root_tile_blocks * n_col)
        ]
        drain(rr_buf.at[pl.ds(0, 2 * rows_all - 1)], recv_sems.at[2])
        for q in range(n_col):
            root_x[q] = jnp.concatenate(
                [
                    jnp.concatenate(
                        [
                            rr_buf[p * rows_all + k][:, q * sep : (q + 1) * sep].astype(F32)
                            for k in range(rows_all)
                        ],
                        1,
                    )
                    for p in range(2)
                ],
                0,
            )
        settle_pair(root_w, 2)
        settle_far(root_w, 2)
        drain(pass_buf.at[pl.ds(0, (2 * rows_all - 1) * n_col)], recv_sems.at[4])

        def pass_value(p, block):
            total = None
            for f in range(2):
                place = places[block][f]
                index = jnp.where(place >= 0, p * rows_all * n_col + place, no_pass)
                value = pass_buf[index].astype(F32)
                total = value if total is None else total + value
            return total

        terms = []
        for c2 in range(n_col):
            passed = jnp.concatenate(
                [
                    jnp.concatenate(
                        [pass_value(p, c2 * root_tile_blocks + b) for b in range(root_tile_blocks)],
                        1,
                    )
                    for p in range(2)
                ],
                0,
            )
            term = contract((root_x[c2] + passed).astype(BF16), lower(root_w, c2), 1, 1)
            if c2 > 0:
                term = jnp.concatenate([jnp.zeros((2 * panel, c2 * sep), F32), term], 1)
            terms.append(term)
        root_forward = add_up(terms)
        totals = []
        for c2 in range(n_col):
            total = contract(
                root_forward[:, c2 * sep :].astype(BF16), lower(root_w, c2), 1, 0
            )
            for b in range(root_tile_blocks):
                solved[c2 * root_tile_blocks + b] = total[
                    :, b * BLOCK_ROWS : (b + 1) * BLOCK_ROWS
                ].astype(BF16)
            totals.append(total)
        for r2 in range(rows_all):
            for q in range(n_col):
                block = solved[child_map[r2 // ranks, q * ranks + r2 % ranks]]
                for p in range(2):
                    known_send[2 * r2 + p, q] = block[p * panel : (p + 1) * panel]
        for m in reversed(range(rows_all)):
            _, r2 = flip(m)
            push(known_send.at[2 * r2 + 1], known_recv.at[r], 5, at(m, across))
            if m:
                push(known_send.at[2 * r2], known_recv.at[r], 5, at(m, c))
        share_across(child_w, 0)
        known_recv[r] = known_send[2 * r]
        for r2 in range(rows_all):
            piece = jnp.concatenate(
                [total[:, r2 * sep : (r2 + 1) * sep] for total in totals], 1
            ).astype(BF16)
            for p in range(2):
                for b in range(piece_blocks):
                    extra_send[2 * r2 + p, b] = piece[
                        p * panel : (p + 1) * panel, b * BLOCK_ROWS : (b + 1) * BLOCK_ROWS
                    ]
        for m in reversed(range(rows_all)):
            _, r2 = flip(m)
            push(extra_send.at[2 * r2 + 1], extra_recv.at[r], 6, at(m, across))
            if m:
                push(extra_send.at[2 * r2], extra_recv.at[r], 6, at(m, c))
        extra_recv[r] = extra_send[2 * r]

    relay(off_w, 1)
    settle_far(off_w, 1)

    def from_root(buffer, phase):
        pl.when(x == 0)(lambda: drain(buffer.at[pl.ds(0, rows_all - 1)], recv_sems.at[phase]))
        pl.when(x == 1)(lambda: drain(buffer, recv_sems.at[phase]))

    from_root(known_recv, 5)
    known = jnp.concatenate(
        [
            add_up([known_recv[k, q].astype(F32) for k in range(rows_all)])
            for q in range(n_col)
        ],
        1,
    ).astype(BF16)
    corrections = [contract(known, flat(off_w, c2), 1, 0) for c2 in range(n_col)]
    for k in range(ranks):
        back_send[k] = jnp.concatenate(
            [term[:, k * sep : (k + 1) * sep] for term in corrections], 1
        ).astype(BF16)

    def rank_of(m):
        _, r2 = flip(m)
        return r2 - front * ranks

    for m in reversed(range(1, ranks)):
        push(back_send.at[rank_of(m)], back_recv.at[rank], 7, at(m, c))
    back_recv[rank] = back_send[rank]
    for q in range(n_col):
        whole_send[q] = known[:, q * BLOCK_ROWS : (q + 1) * BLOCK_ROWS]
    for m in reversed(range(1, ranks)):
        push(whole_send, whole_recv.at[pl.ds(rank * n_col, n_col)], 9, at(m, c))
    whole_recv[pl.ds(rank * n_col, n_col)] = whole_send[...]
    relay(child_w, 0)
    own = jnp.concatenate([forward_own[q].astype(F32) for q in range(n_col)], 1)
    settle_far(child_w, 0)
    drain(back_recv.at[pl.ds(0, ranks - 1)], recv_sems.at[7])
    back = own - add_up([back_recv[k].astype(F32) for k in range(ranks)])
    totals = []
    for c2 in range(n_col):
        total = contract(back[:, c2 * sep :].astype(BF16), lower(child_w, c2), 1, 0)
        for b in range(child_tile_blocks):
            final_blocks[c2 * child_tile_blocks + b] = total[
                :, b * BLOCK_ROWS : (b + 1) * BLOCK_ROWS
            ].astype(BF16)
        totals.append(total)
    for k in range(ranks):
        for q in range(n_col):
            block = subtree_map[2 * front + k // n_row, q * n_row + k % n_row]
            final_send[k, q] = final_blocks[jnp.minimum(block, sep_blocks - 1)]
        piece = jnp.concatenate(
            [total[:, k * sep : (k + 1) * sep] for total in totals], 1
        ).astype(BF16)
        for b in range(piece_blocks):
            final_send[k, n_col + b] = piece[:, b * BLOCK_ROWS : (b + 1) * BLOCK_ROWS]
    for m in reversed(range(1, ranks)):
        push(final_send.at[rank_of(m)], final_recv.at[rank], 8, at(m, c))
    final_recv[rank] = final_send[rank]

    def piece_of(buffer, count, first):
        total = jnp.concatenate(
            [
                add_up([buffer[k, first + b].astype(F32) for k in range(count)])
                for b in range(piece_blocks)
            ],
            1,
        )
        return total.reshape(panel, n_col, sep)

    from_root(extra_recv, 6)
    root_out[...] = piece_of(extra_recv, rows_all, 0)
    drain(whole_recv.at[pl.ds(0, (ranks - 1) * n_col)], recv_sems.at[9])
    drain(final_recv.at[pl.ds(0, ranks - 1)], recv_sems.at[8])
    child_out[...] = piece_of(final_recv, ranks, n_col)
    for q in range(n_col):
        block = subtree_map[leaf, q * n_row + row]
        total = add_up([final_recv[k, q].astype(F32) for k in range(ranks)])
        j = jnp.maximum(block - sep_blocks, 0)
        whole = whole_recv[lax.rem(j, ranks) * n_col + lax.div(j, ranks)]
        leaf_out[:, q, :] = jnp.where(block < sep_blocks, total.astype(BF16), whole)

    drain(rhs_recv.at[pl.ds(0, (group - 1) * rhs_width)], send_sems.at[0])
    drain(fwd_recv.at[pl.ds(0, group - 1)], send_sems.at[1])
    drain(rr_buf.at[pl.ds(0, rows_all - 1)], send_sems.at[2])
    drain(half_send, send_sems.at[3])
    drain(back_recv.at[pl.ds(0, ranks - 1)], send_sems.at[7])
    drain(final_recv.at[pl.ds(0, ranks - 1)], send_sems.at[8])
    drain(whole_recv.at[pl.ds(0, (ranks - 1) * n_col)], send_sems.at[9])
    conclude(child_w, 0, 0, c)
    conclude(child_w, 0, 1, c)
    conclude(child_w, 0, 2, across)
    conclude(off_w, 1, 0, c)
    conclude(off_w, 1, 1, c)
    conclude(off_w, 1, 2, across)

    @pl.when(x == 0)
    def _():
        drain(pass_buf.at[pl.ds(0, (rows_all - 1) * n_col)], send_sems.at[4])
        drain(known_send.at[pl.ds(0, 2 * rows_all - 1)], send_sems.at[5])
        drain(extra_send.at[pl.ds(0, 2 * rows_all - 1)], send_sems.at[6])
        conclude(root_w, 2, 1, c)
        conclude(root_w, 2, 2, across)

    @pl.when(x == 1)
    def _():
        drain(rr_send, send_sems.at[2])
        conclude(root_w, 2, 0, c)


def place_kernel(*refs):
    copies = [
        pltpu.make_async_copy(refs[k], refs[3 + k], refs[6].at[k]) for k in range(3)
    ]
    for copy in copies:
        copy.start()
    for copy in copies:
        copy.wait()


def fused(
    rhs_root, rhs_child, subtree_update, inv_root, inv_child, off_child, child_map, subtree_map
):
    n_col = lax.axis_size("col")
    n_row = lax.axis_size("row")
    n_leaf = lax.axis_size("leaf")
    panel = rhs_child.shape[0]
    sep = rhs_child.shape[2]
    ranks = n_row * (n_leaf // 2)
    rows_all = n_leaf * n_row
    group = 2 * ranks
    root_width = inv_root.shape[2]
    child_width = inv_child.shape[2]
    sep_blocks = child_width * n_col // BLOCK_ROWS
    root_blocks = root_width * n_col // BLOCK_ROWS
    piece = n_col * sep
    mixed = n_col + piece // BLOCK_ROWS

    vmem = pl.BlockSpec(memory_space=pltpu.VMEM)
    hbm = pl.BlockSpec(memory_space=pl.ANY)
    buffer = lambda *shape: pltpu.VMEM(shape, BF16)
    outs = pl.pallas_call(
        solve_kernel,
        out_shape=(
            jax.ShapeDtypeStruct((panel, n_col, sep), F32),
            jax.ShapeDtypeStruct((panel, n_col, sep), F32),
            jax.ShapeDtypeStruct((panel, n_col, BLOCK_ROWS), BF16),
        ),
        in_specs=[hbm] * 8,
        out_specs=(vmem, vmem, vmem),
        scratch_shapes=[
            pltpu.SMEM(child_map.shape, jnp.int32), pltpu.SMEM(subtree_map.shape, jnp.int32),
            buffer(*subtree_update.shape), buffer(*rhs_child.shape), buffer(*rhs_root.shape),
            buffer(n_col, *inv_root.shape), buffer(n_col, *inv_child.shape),
            buffer(n_col, *off_child.shape),
            buffer(2, n_col + 2, panel, BLOCK_ROWS),
            buffer(group * (n_col + 2) + 1, panel, BLOCK_ROWS),
            buffer(panel, piece), buffer(2 * rows_all, panel, piece),
            buffer(2, 2, 2 * panel, sep), buffer(group, 2, 2 * panel, sep),
            buffer(n_col + 2, panel, BLOCK_ROWS), buffer(n_col + 2, panel, BLOCK_ROWS),
            pltpu.VMEM((2, n_col, panel, BLOCK_ROWS), F32), buffer(n_col, panel, sep),
            buffer(n_col, panel, BLOCK_ROWS), buffer(2 * rows_all * n_col + 1, panel, BLOCK_ROWS),
            pltpu.VMEM((n_col, 2 * panel, root_width), F32),
            buffer(root_blocks, 2 * panel, BLOCK_ROWS),
            buffer(2 * rows_all, n_col, panel, BLOCK_ROWS),
            buffer(rows_all, n_col, panel, BLOCK_ROWS),
            buffer(2 * rows_all, piece // BLOCK_ROWS, panel, BLOCK_ROWS),
            buffer(rows_all, piece // BLOCK_ROWS, panel, BLOCK_ROWS),
            buffer(n_col, panel, BLOCK_ROWS), buffer(ranks * n_col, panel, BLOCK_ROWS),
            buffer(ranks, panel, piece), buffer(ranks, panel, piece),
            buffer(sep_blocks, panel, BLOCK_ROWS),
            buffer(ranks, mixed, panel, BLOCK_ROWS), buffer(ranks, mixed, panel, BLOCK_ROWS),
            pltpu.SemaphoreType.DMA((8,)),
            pltpu.SemaphoreType.DMA((10,)),
            pltpu.SemaphoreType.DMA((10,)),
            pltpu.SemaphoreType.DMA((3, 3, 4)),
            pltpu.SemaphoreType.DMA((3, 3, 4)),
        ],
        compiler_params=pltpu.CompilerParams(
            collective_id=0, has_side_effects=True, vmem_limit_bytes=60 * 1024 * 1024
        ),
    )(
        child_map, subtree_map, subtree_update, rhs_child, rhs_root, inv_root, inv_child, off_child,
    )
    return pl.pallas_call(
        place_kernel,
        out_shape=tuple(jax.ShapeDtypeStruct(out.shape, out.dtype) for out in outs),
        in_specs=[vmem] * 3,
        out_specs=(hbm,) * 3,
        scratch_shapes=[pltpu.SemaphoreType.DMA((3,))],
    )(*outs)


def body(*arrays):
    whole_blocks = (
        lax.axis_size("leaf") == 4
        and lax.axis_size("row") == 2
        and lax.axis_size("col") == 4
        and arrays[2].shape[2] == BLOCK_ROWS
        and arrays[4].shape[2] % BLOCK_ROWS == 0
        and arrays[0].shape[0] % 16 == 0
        and arrays[0].shape[2] % 16 == 0
        and arrays[0].shape[2] <= BLOCK_ROWS
        and arrays[0].shape[1] * arrays[0].shape[2] % BLOCK_ROWS == 0
    )
    return (fused if whole_blocks else local)(*arrays)


def solution(mesh):
    in_specs = (
        P("col", None, ("leaf", "row")),
        P("col", None, ("leaf", "row")),
        P("col", None, ("leaf", "row")),
        P(None, ("leaf", "row"), "col"),
        P(None, ("leaf", "row"), "col"),
        P(None, ("leaf", "row"), "col"),
        P(),
        P(),
    )
    out_specs = (
        P("col", None, ("leaf", "row")),
        P("col", None, ("leaf", "row")),
        P("col", None, ("leaf", "row")),
    )
    return jax.shard_map(body, mesh=mesh, in_specs=in_specs, out_specs=out_specs, check_vma=False)
```

```python
import functools

import jax
import jax.numpy as jnp
from jax import lax
from jax.experimental import pallas as pl
from jax.experimental.pallas import tpu as pltpu
from jax.sharding import PartitionSpec as P

BLOCK_ROWS = 128


def partner_2(block, axis, bit):
    count = lax.axis_size(axis)
    route = []
    for low in range(count):
        high = low | 1 << bit
        if high != low and high < count:
            route += [(low, high), (high, low)]
    return lax.ppermute(block, axis, route)


def group_gather(piece, group_size):
    merged = lax.all_gather(piece, "row", axis=2, tiled=True)
    leaf_index = lax.axis_index("leaf")
    for bit_number in range(group_size.bit_length() - 1):
        partner = partner_2(merged, "leaf", bit_number)
        upper = leaf_index >> bit_number & 1 == 1
        merged = jnp.where(
            upper, jnp.concatenate([partner, merged], 2), jnp.concatenate([merged, partner], 2)
        )
    return merged


def group_sum(partial_sum, group_size):
    leaf_index = lax.axis_index("leaf")
    for bit_number in reversed(range(group_size.bit_length() - 1)):
        middle = partial_sum.shape[1] // 2
        lower_half = partial_sum[:, :middle]
        upper_half = partial_sum[:, middle:]
        upper = leaf_index >> bit_number & 1 == 1
        outgoing = jnp.where(upper, lower_half, upper_half)
        kept_half = jnp.where(upper, upper_half, lower_half)
        partial_sum = kept_half + partner_2(
            outgoing.astype(jnp.bfloat16), "leaf", bit_number
        ).astype(outgoing.dtype)
    return lax.psum_scatter(
        partial_sum.astype(jnp.bfloat16), "row", scatter_dimension=1, tiled=True
    ).astype(jnp.float32)


def one_hot(block_map, blocks_total):
    return (block_map[..., None] == jnp.arange(blocks_total, dtype=jnp.int32)).astype(jnp.bfloat16)


def pick_piece(source, position, along):
    return lax.dynamic_index_in_dim(source, position, along, keepdims=False)


def contract(left_side, right_side, left_dim, right_dim):
    return lax.dot_general(
        left_side,
        right_side,
        (((left_dim,), (right_dim,)), ((), ())),
        preferred_element_type=jnp.float32,
    )


def local(
    rhs_root, rhs_child, subtree_update, inv_root, inv_child, off_child, child_map, subtree_map
):
    n_col = lax.axis_size("col")
    n_row = lax.axis_size("row")
    n_leaf = lax.axis_size("leaf")
    group_size = n_leaf // 2
    sub_size = n_leaf // 4
    col_index = lax.axis_index("col")
    leaf_index = lax.axis_index("leaf")
    row_index = lax.axis_index("row")
    front_index = leaf_index // group_size
    member = leaf_index % group_size
    child_rank = member * n_row + row_index
    half_index = member // sub_size
    sub_rank = member % sub_size * n_row + row_index
    panel_width = rhs_child.shape[0]
    right_sides = panel_width * n_col
    sep_piece = rhs_child.shape[2]
    upd_piece = subtree_update.shape[2]
    root_width = inv_root.shape[2]
    child_width = inv_child.shape[2]
    child_order = child_width * n_col
    child_update = upd_piece * n_col * group_size * n_row
    root_blocks = root_width * n_col // BLOCK_ROWS
    child_blocks = (child_order + child_update) // BLOCK_ROWS
    root_matrix = inv_root.reshape(n_col * sep_piece, root_width)
    child_matrix = inv_child.reshape(n_col * sep_piece, child_width)
    off_matrix = off_child.reshape(n_col * upd_piece, child_width)
    joined = jnp.concatenate([subtree_update, rhs_child], 2)
    gathered = group_gather(joined, group_size).reshape(
        panel_width, n_col, group_size * n_row, upd_piece + sep_piece
    )
    sub_vectors = (
        gathered[..., :upd_piece]
        .reshape(panel_width, n_col, 2, -1)
        .transpose(2, 0, 1, 3)
        .reshape(2, panel_width, -1, BLOCK_ROWS)
    )
    child_rhs_full = gathered[..., upd_piece:].reshape(panel_width, child_order)
    sub_rows = lax.dynamic_slice_in_dim(subtree_map, 2 * front_index, 2, 0)
    spread = jnp.einsum(
        "hpjt,hjn->pnt",
        sub_vectors,
        one_hot(sub_rows, child_blocks),
        preferred_element_type=jnp.float32,
    ).reshape(panel_width, -1)
    child_sep = (spread[:, :child_order] + child_rhs_full.astype(jnp.float32)).astype(jnp.bfloat16)
    child_tail = spread[:, child_order:]
    child_tile = lax.all_to_all(
        child_sep.reshape(panel_width, n_col, child_width),
        "col",
        split_axis=1,
        concat_axis=0,
        tiled=True,
    ).reshape(right_sides, child_width)
    child_forward = lax.psum(contract(child_tile, child_matrix, 1, 1), "col").astype(jnp.bfloat16)
    forward_quarter = lax.dynamic_slice_in_dim(
        child_forward.reshape(right_sides, n_col, sep_piece), col_index, 1, 1
    )
    forward_tile = group_gather(forward_quarter, group_size).reshape(right_sides, child_width)
    pass_term = lax.psum_scatter(
        contract(forward_tile, off_matrix, 1, 1), "col", scatter_dimension=0, tiled=True
    )
    tail_mine = pick_piece(
        child_tail.reshape(panel_width, n_col, group_size * n_row, upd_piece), child_rank, 2
    )
    child_pass = (tail_mine - pass_term.reshape(panel_width, n_col, upd_piece)).astype(jnp.bfloat16)
    joined_root = jnp.concatenate([child_pass, rhs_root], 2)
    root_all = lax.all_gather(joined_root, ("leaf", "row"), axis=2, tiled=True).reshape(
        panel_width, n_col, n_leaf * n_row, upd_piece + sep_piece
    )
    pass_vectors = (
        root_all[..., :upd_piece]
        .reshape(panel_width, n_col, 2, -1)
        .transpose(2, 0, 1, 3)
        .reshape(2, panel_width, -1, BLOCK_ROWS)
    )
    root_rhs_full = root_all[..., upd_piece:].reshape(panel_width, root_width * n_col)
    root_spread = jnp.einsum(
        "hpjt,hjn->pnt",
        pass_vectors,
        one_hot(child_map, root_blocks),
        preferred_element_type=jnp.float32,
    ).reshape(panel_width, -1)
    root_sep = (root_spread + root_rhs_full.astype(jnp.float32)).astype(jnp.bfloat16)
    root_tile = lax.all_to_all(
        root_sep.reshape(panel_width, n_col, root_width),
        "col",
        split_axis=1,
        concat_axis=0,
        tiled=True,
    ).reshape(right_sides, root_width)
    root_forward = lax.psum(contract(root_tile, root_matrix, 1, 1), "col").astype(jnp.bfloat16)
    map_row = pick_piece(child_map, front_index, 0)
    root_piece = lax.psum_scatter(
        contract(root_matrix, root_forward, 0, 1), ("leaf", "row"), scatter_dimension=0, tiled=True
    )
    solution_root = lax.all_to_all(
        root_piece.T.reshape(right_sides, 1, sep_piece),
        "col",
        split_axis=0,
        concat_axis=1,
        tiled=True,
    )
    root_everywhere = lax.all_gather(
        solution_root.astype(jnp.bfloat16), ("leaf", "row"), axis=2, tiled=True
    ).reshape(panel_width, root_blocks, BLOCK_ROWS)
    known_full = (
        jnp.einsum(
            "pnt,jn->pjt",
            root_everywhere,
            one_hot(map_row, root_blocks),
            preferred_element_type=jnp.float32,
        )
        .astype(jnp.bfloat16)
        .reshape(panel_width, child_update)
    )
    known_mine = pick_piece(
        known_full.reshape(panel_width, n_col, group_size * n_row, upd_piece), child_rank, 2
    )
    known_rows = lax.all_gather(known_mine, "col", axis=0, tiled=True).reshape(
        right_sides, n_col * upd_piece
    )
    correction = group_sum(contract(known_rows, off_matrix, 1, 0), group_size)
    back_quarter = (
        forward_quarter.reshape(right_sides, sep_piece).astype(jnp.float32) - correction
    ).astype(jnp.bfloat16)
    back_rows = lax.all_gather(
        back_quarter.reshape(right_sides, 1, sep_piece), "col", axis=1, tiled=True
    ).reshape(right_sides, n_col * sep_piece)
    child_piece = group_sum(contract(back_rows, child_matrix, 1, 0), group_size)
    solution_child = lax.all_to_all(
        child_piece.reshape(right_sides, 1, sep_piece),
        "col",
        split_axis=0,
        concat_axis=1,
        tiled=True,
    )
    child_rounded = solution_child.astype(jnp.bfloat16)
    sep_whole = group_gather(child_rounded, group_size).reshape(panel_width, child_order)
    child_whole = jnp.concatenate([sep_whole, known_full], 1)
    sub_row = pick_piece(subtree_map, 2 * front_index + half_index, 0)
    leaf_full = jnp.einsum(
        "pnt,jn->pjt",
        child_whole.reshape(panel_width, child_blocks, BLOCK_ROWS),
        one_hot(sub_row, child_blocks),
        preferred_element_type=jnp.float32,
    ).astype(jnp.bfloat16)
    leaf_solution = pick_piece(
        leaf_full.reshape(panel_width, n_col, sub_size * n_row, upd_piece), sub_rank, 2
    )
    return (solution_root, solution_child, leaf_solution)


F32 = jnp.float32
BF16 = jnp.bfloat16


def add_up(terms):
    total = terms[0]
    for term in terms[1:]:
        total = total + term
    return total


def solve_kernel(
    child_hbm_map, subtree_hbm_map, sub_hbm, rc_hbm, rr_hbm, root_hbm, child_hbm, off_hbm,
    root_out, child_out, leaf_out,
    child_map, subtree_map, sub_in, rc_in, rr_in,
    root_w, child_w, off_w,
    rhs_send, rhs_recv, rr_send, rr_buf,
    fwd_send, fwd_recv, half_send, half_recv, half_own, forward_own,
    pass_send, pass_buf, root_x, solved,
    known_send, known_recv, extra_send, extra_recv,
    whole_send, whole_recv, back_send, back_recv, final_blocks, final_send, final_recv,
    load_sems, send_sems, recv_sems, share_sems, shared_sems,
):
    n_leaf, n_row, n_col = lax.axis_size("leaf"), lax.axis_size("row"), lax.axis_size("col")
    panel = sub_in.shape[0]
    sep = rc_in.shape[2]
    ranks = n_row * (n_leaf // 2)
    rows_all = n_leaf * n_row
    child_tile_blocks = child_w.shape[3] // BLOCK_ROWS
    root_tile_blocks = root_w.shape[3] // BLOCK_ROWS
    sep_blocks = child_tile_blocks * n_col
    piece_blocks = n_col * sep // BLOCK_ROWS
    c = lax.axis_index("col")
    leaf = lax.axis_index("leaf")
    row = lax.axis_index("row")
    x = lax.div(c, 2)
    core = lax.rem(c, 2)
    front = lax.div(leaf, 2)
    low = lax.rem(leaf, 2)
    rank = low * n_row + row
    r = leaf * n_row + row
    pair = 2 * x + 1 - core
    across = 2 * (1 - x) + core
    far = 2 * (1 - x) + 1 - core

    loads = [
        pltpu.make_async_copy(source, target, load_sems.at[number])
        for number, (source, target) in enumerate((
            (sub_hbm, sub_in), (rc_hbm, rc_in),
            (subtree_hbm_map, subtree_map), (child_hbm_map, child_map),
            (child_hbm, child_w.at[c]), (root_hbm, root_w.at[c]),
            (off_hbm, off_w.at[c]), (rr_hbm, rr_in),
        ))
    ]
    for load in loads:
        load.start()

    def flip(m):
        other_leaf = 2 * (1 - front if m & 4 else front) + (1 - low if m & 2 else low)
        other_row = 1 - row if m & 1 else row
        return {"leaf": other_leaf, "row": other_row}, other_leaf * n_row + other_row

    def at(m, c2):
        place, _ = flip(m)
        return {**place, "col": c2}

    def push(source, target, phase, device):
        pltpu.make_async_remote_copy(
            src_ref=source,
            dst_ref=target,
            send_sem=send_sems.at[phase],
            recv_sem=recv_sems.at[phase],
            device_id=device,
            device_id_type=pl.DeviceIdType.MESH,
        ).start()

    def drain(view, sem):
        pltpu.make_async_copy(view, view, sem).wait()

    barrier = pltpu.get_barrier_semaphore()

    def greet(device):
        pl.semaphore_signal(
            barrier, inc=1, device_id=device, device_id_type=pl.DeviceIdType.MESH
        )

    def tiles_of(full, c2, body, tiles=(3, 2, 1, 0)):
        for q in tiles:
            if full:
                body(q)
            else:
                pl.when(q >= c2)(functools.partial(body, q))

    def hand(weights, slot, q, number, kind, c2):
        pltpu.make_async_remote_copy(
            src_ref=weights.at[slot, q],
            dst_ref=weights.at[slot, q],
            send_sem=share_sems.at[number, kind, q],
            recv_sem=shared_sems.at[number, kind, q],
            device_id={"leaf": leaf, "row": row, "col": c2},
            device_id_type=pl.DeviceIdType.MESH,
        ).start()

    def share_across(weights, number, tiles=(3, 2, 1, 0)):
        tiles_of(number == 1, c, lambda q: hand(weights, c, q, number, 0, across), tiles)

    def share_pair(weights, number):
        tiles_of(number < 2, c, lambda q: hand(weights, c, q, number, 1, pair))

    def settle_pair(weights, number):
        tiles_of(number < 2, pair, lambda q: drain(weights.at[0, q], shared_sems.at[number, 1, q]))

    def relay(weights, number):
        def pass_on(q):
            drain(weights.at[across, q], shared_sems.at[number, 0, q])
            hand(weights, across, q, number, 2, pair)

        tiles_of(number == 1, across, pass_on)

    def settle_far(weights, number):
        tiles_of(number == 1, far, lambda q: drain(weights.at[0, q], shared_sems.at[number, 2, q]))

    def conclude(weights, number, kind, slot):
        full = number == 1 or (number == 0 and kind == 1)
        tiles_of(full, slot, lambda q: drain(weights.at[0, q], share_sems.at[number, kind, q]))

    def lower(weights, c2):
        return weights[c2, c2:].reshape(-1, weights.shape[3])

    def flat(weights, c2):
        return weights[c2].reshape(-1, weights.shape[3])

    for m in range(rows_all):
        if m > 0:
            greet(at(m, c))
        greet(at(m, across))
    greet(at(0, pair))

    loads[0].wait()
    loads[1].wait()
    loads[7].wait()
    pad = jnp.zeros((panel, BLOCK_ROWS - sep), BF16)
    for q in range(n_col):
        value = sub_in[:, q, :]
        for half in range(2):
            rhs_send[half, q] = value
        rhs_send[q // 2, n_col + q % 2] = jnp.concatenate([rc_in[:, q, :], pad], 1)
    rr_send[...] = jnp.concatenate([rr_in[:, q, :] for q in range(n_col)], 1)
    rhs_width = rhs_send.shape[1]
    group = 2 * ranks
    no_rhs = group * rhs_width
    no_pass = 2 * rows_all * n_col
    rhs_recv[no_rhs] = jnp.zeros((panel, BLOCK_ROWS), BF16)
    pass_buf[no_pass] = jnp.zeros((panel, BLOCK_ROWS), BF16)
    pl.semaphore_wait(barrier, 2 * rows_all)

    for side in (1, 0):
        for m in reversed(range(ranks)):
            if side or m:
                half = 1 - x if side else x
                push(
                    rhs_send.at[half],
                    rhs_recv.at[pl.ds((x * ranks + rank) * rhs_width, rhs_width)],
                    0,
                    at(m, across if side else c),
                )
    rhs_recv[pl.ds((x * ranks + rank) * rhs_width, rhs_width)] = rhs_send[x]
    loads[4].wait()
    share_pair(child_w, 0)
    loads[5].wait()
    loads[6].wait()
    share_pair(off_w, 1)

    @pl.when(x == 0)
    def _():
        rr_buf[r] = rr_send[...]

    @pl.when(x == 1)
    def _():
        share_across(root_w, 2)

    loads[2].wait()
    loads[3].wait()
    targets = [
        [subtree_map[2 * front + h, j] for j in range(subtree_map.shape[1])] for h in range(2)
    ]

    def sub_place(h, block):
        place = -1
        for j, target in enumerate(targets[h]):
            source = (h * n_row + j % n_row) * rhs_width + j // n_row
            place = jnp.where(target == block, source, place)
        return place

    def sub_value(p, place):
        index = jnp.where(place >= 0, p * ranks * rhs_width + place, no_rhs)
        return rhs_recv[index].astype(F32)

    half_places = [
        [[sub_place(h, (2 * x + i) * child_tile_blocks + b) for h in range(2)]
         for b in range(child_tile_blocks)]
        for i in range(2)
    ]
    drain(rhs_recv.at[pl.ds(0, (group - 1) * rhs_width)], recv_sems.at[0])
    settle_pair(child_w, 0)
    partial_sum = None
    for i in range(2):
        rows = []
        for p in range(2):
            rhs = jnp.concatenate(
                [
                    rhs_recv[(p * ranks + k) * rhs_width + n_col + i][:, :sep].astype(F32)
                    for k in range(ranks)
                ],
                1,
            )
            placed = jnp.concatenate(
                [
                    sub_value(p, half_places[i][b][0]) + sub_value(p, half_places[i][b][1])
                    for b in range(child_tile_blocks)
                ],
                1,
            )
            rows.append(rhs + placed)
        term = contract(
            jnp.concatenate(rows, 0).astype(BF16), flat(child_w, 2 * x + i), 1, 1
        )
        partial_sum = term if partial_sum is None else partial_sum + term
    for q in range(n_col):
        fwd_send[q // 2, q % 2] = partial_sum[:, q * sep : (q + 1) * sep].astype(BF16)

    for side in (1, 0):
        for m in reversed(range(ranks)):
            if side or m:
                half = 1 - x if side else x
                push(
                    fwd_send.at[half], fwd_recv.at[x * ranks + rank], 1,
                    at(m, across if side else c),
                )
    fwd_recv[x * ranks + rank] = fwd_send[x]

    @pl.when(x == 0)
    def _():
        pass

    @pl.when(x == 1)
    def _():
        pass

    tail = []
    for q in range(n_col):
        block = sep_blocks + q * ranks + rank
        tail.append(sub_value(x, sub_place(0, block)) + sub_value(x, sub_place(1, block)))
    settle_pair(off_w, 1)
    drain(fwd_recv.at[pl.ds(0, group - 1)], recv_sems.at[1])
    z = None
    for i in range(2):
        y = jnp.concatenate(
            [
                fwd_recv[k, i].astype(F32) + fwd_recv[ranks + k, i].astype(F32)
                for k in range(ranks)
            ],
            1,
        ).astype(BF16)
        term = contract(y, flat(off_w, 2 * x + i), 1, 1)
        z = term if z is None else z + term
    for p in range(2):
        for q in range(n_col):
            half_own[p, q] = z[p * panel : (p + 1) * panel, q * BLOCK_ROWS : (q + 1) * BLOCK_ROWS]
    for q in range(n_col):
        half_send[q] = half_own[1 - x, q].astype(BF16)
    for i in range(2):
        mine = (fwd_recv[rank, i].astype(F32) + fwd_recv[ranks + rank, i].astype(F32)).astype(BF16)
        other = jnp.where(x == 0, mine[panel:], mine[:panel])
        half_send[n_col + i] = jnp.concatenate([other, pad], 1)
        forward_own[2 * x + i] = jnp.where(x == 0, mine[:panel], mine[panel:])
    push(half_send, half_recv, 3, at(0, across))
    pl.when(x == 0)(lambda: share_pair(root_w, 2))
    pl.when(x == 0)(lambda: share_across(off_w, 1))
    for m in reversed(range(rows_all)):
        if m:
            push(rr_send, rr_buf.at[x * rows_all + r], 2, at(m, core))
    pl.when(x == 1)(lambda: push(rr_send, rr_buf.at[rows_all + r], 2, at(0, core)))

    drain(half_recv, recv_sems.at[3])
    pl.when(x == 0)(lambda: relay(root_w, 2))
    for q in range(n_col):
        total = half_own[x, q] + half_recv[q].astype(F32)
        pass_send[q] = (tail[q] - total).astype(BF16)
    for m in reversed(range(rows_all)):
        if m:
            push(pass_send, pass_buf.at[pl.ds((x * rows_all + r) * n_col, n_col)], 4, at(m, core))

    @pl.when(x == 1)
    def _():
        push(pass_send, pass_buf.at[pl.ds((rows_all + r) * n_col, n_col)], 4, at(0, core))
        drain(pass_buf.at[pl.ds(0, rows_all * n_col)], send_sems.at[4])
        share_across(off_w, 1)
        share_across(child_w, 0)

    for i in range(2):
        forward_own[2 * (1 - x) + i] = half_recv[n_col + i][:, :sep]

    @pl.when(x == 0)
    def _():
        pass_buf[pl.ds(r * n_col, n_col)] = pass_send[...]
        maps = [[child_map[f, j] for j in range(child_map.shape[1])] for f in range(2)]

        def pass_place(f, block):
            place = -1
            for j, target in enumerate(maps[f]):
                source = (f * ranks + j % ranks) * n_col + j // ranks
                place = jnp.where(target == block, source, place)
            return place

        places = [
            [pass_place(f, block) for f in range(2)] for block in range(root_tile_blocks * n_col)
        ]
        drain(rr_buf.at[pl.ds(0, 2 * rows_all - 1)], recv_sems.at[2])
        for q in range(n_col):
            root_x[q] = jnp.concatenate(
                [
                    jnp.concatenate(
                        [
                            rr_buf[p * rows_all + k][:, q * sep : (q + 1) * sep].astype(F32)
                            for k in range(rows_all)
                        ],
                        1,
                    )
                    for p in range(2)
                ],
                0,
            )
        settle_pair(root_w, 2)
        settle_far(root_w, 2)
        drain(pass_buf.at[pl.ds(0, (2 * rows_all - 1) * n_col)], recv_sems.at[4])

        def pass_value(p, block):
            total = None
            for f in range(2):
                place = places[block][f]
                index = jnp.where(place >= 0, p * rows_all * n_col + place, no_pass)
                value = pass_buf[index].astype(F32)
                total = value if total is None else total + value
            return total

        terms = []
        for c2 in range(n_col):
            passed = jnp.concatenate(
                [
                    jnp.concatenate(
                        [pass_value(p, c2 * root_tile_blocks + b) for b in range(root_tile_blocks)],
                        1,
                    )
                    for p in range(2)
                ],
                0,
            )
            term = contract((root_x[c2] + passed).astype(BF16), lower(root_w, c2), 1, 1)
            if c2 > 0:
                term = jnp.concatenate([jnp.zeros((2 * panel, c2 * sep), F32), term], 1)
            terms.append(term)
        root_forward = add_up(terms)
        totals = []
        for c2 in range(n_col):
            total = contract(
                root_forward[:, c2 * sep :].astype(BF16), lower(root_w, c2), 1, 0
            )
            for b in range(root_tile_blocks):
                solved[c2 * root_tile_blocks + b] = total[
                    :, b * BLOCK_ROWS : (b + 1) * BLOCK_ROWS
                ].astype(BF16)
            totals.append(total)
        for m in reversed(range(rows_all)):
            _, r2 = flip(m)
            f2 = lax.div(r2, ranks)
            for q in range(n_col):
                block = solved[child_map[f2, q * ranks + r2 - f2 * ranks]]
                for p in range(2):
                    known_send[2 * r2 + p, q] = block[p * panel : (p + 1) * panel]
            if m:
                push(known_send.at[2 * r2], known_recv.at[r], 5, at(m, c))
            push(known_send.at[2 * r2 + 1], known_recv.at[r], 5, at(m, across))
        share_across(child_w, 0)
        known_recv[r] = known_send[2 * r]
        for r2 in range(rows_all):
            piece = jnp.concatenate(
                [total[:, r2 * sep : (r2 + 1) * sep] for total in totals], 1
            ).astype(BF16)
            for p in range(2):
                for b in range(piece_blocks):
                    extra_send[2 * r2 + p, b] = piece[
                        p * panel : (p + 1) * panel, b * BLOCK_ROWS : (b + 1) * BLOCK_ROWS
                    ]
        for m in reversed(range(rows_all)):
            _, r2 = flip(m)
            push(extra_send.at[2 * r2 + 1], extra_recv.at[r], 6, at(m, across))
            if m:
                push(extra_send.at[2 * r2], extra_recv.at[r], 6, at(m, c))
        extra_recv[r] = extra_send[2 * r]

    relay(off_w, 1)
    settle_far(off_w, 1)

    def from_root(buffer, phase):
        pl.when(x == 0)(lambda: drain(buffer.at[pl.ds(0, rows_all - 1)], recv_sems.at[phase]))
        pl.when(x == 1)(lambda: drain(buffer, recv_sems.at[phase]))

    from_root(known_recv, 5)
    known = jnp.concatenate(
        [
            add_up([known_recv[k, q].astype(F32) for k in range(rows_all)])
            for q in range(n_col)
        ],
        1,
    ).astype(BF16)
    corrections = [contract(known, flat(off_w, c2), 1, 0) for c2 in range(n_col)]
    for k in range(ranks):
        back_send[k] = jnp.concatenate(
            [term[:, k * sep : (k + 1) * sep] for term in corrections], 1
        ).astype(BF16)

    def rank_of(m):
        _, r2 = flip(m)
        return r2 - front * ranks

    for m in reversed(range(1, ranks)):
        push(back_send.at[rank_of(m)], back_recv.at[rank], 7, at(m, c))
    back_recv[rank] = back_send[rank]
    for q in range(n_col):
        whole_send[q] = known[:, q * BLOCK_ROWS : (q + 1) * BLOCK_ROWS]
    for m in reversed(range(1, ranks)):
        push(whole_send, whole_recv.at[pl.ds(rank * n_col, n_col)], 9, at(m, c))
    whole_recv[pl.ds(rank * n_col, n_col)] = whole_send[...]
    relay(child_w, 0)
    own = jnp.concatenate([forward_own[q].astype(F32) for q in range(n_col)], 1)
    settle_far(child_w, 0)
    drain(back_recv.at[pl.ds(0, ranks - 1)], recv_sems.at[7])
    back = own - add_up([back_recv[k].astype(F32) for k in range(ranks)])
    totals = []
    for c2 in range(n_col):
        total = contract(back[:, c2 * sep :].astype(BF16), lower(child_w, c2), 1, 0)
        for b in range(child_tile_blocks):
            final_blocks[c2 * child_tile_blocks + b] = total[
                :, b * BLOCK_ROWS : (b + 1) * BLOCK_ROWS
            ].astype(BF16)
        totals.append(total)
    for k in range(ranks):
        for q in range(n_col):
            block = subtree_map[2 * front + k // n_row, q * n_row + k % n_row]
            final_send[k, q] = final_blocks[jnp.minimum(block, sep_blocks - 1)]
        piece = jnp.concatenate(
            [total[:, k * sep : (k + 1) * sep] for total in totals], 1
        ).astype(BF16)
        for b in range(piece_blocks):
            final_send[k, n_col + b] = piece[:, b * BLOCK_ROWS : (b + 1) * BLOCK_ROWS]
    for m in reversed(range(1, ranks)):
        push(final_send.at[rank_of(m)], final_recv.at[rank], 8, at(m, c))
    final_recv[rank] = final_send[rank]

    def piece_of(buffer, count, first):
        total = jnp.concatenate(
            [
                add_up([buffer[k, first + b].astype(F32) for k in range(count)])
                for b in range(piece_blocks)
            ],
            1,
        )
        return total.reshape(panel, n_col, sep)

    from_root(extra_recv, 6)
    root_out[...] = piece_of(extra_recv, rows_all, 0)
    drain(whole_recv.at[pl.ds(0, (ranks - 1) * n_col)], recv_sems.at[9])
    drain(final_recv.at[pl.ds(0, ranks - 1)], recv_sems.at[8])
    child_out[...] = piece_of(final_recv, ranks, n_col)
    for q in range(n_col):
        block = subtree_map[leaf, q * n_row + row]
        total = add_up([final_recv[k, q].astype(F32) for k in range(ranks)])
        j = jnp.maximum(block - sep_blocks, 0)
        whole = whole_recv[lax.rem(j, ranks) * n_col + lax.div(j, ranks)]
        leaf_out[:, q, :] = jnp.where(block < sep_blocks, total.astype(BF16), whole)

    drain(rhs_recv.at[pl.ds(0, (group - 1) * rhs_width)], send_sems.at[0])
    drain(fwd_recv.at[pl.ds(0, group - 1)], send_sems.at[1])
    drain(rr_buf.at[pl.ds(0, rows_all - 1)], send_sems.at[2])
    drain(half_send, send_sems.at[3])
    drain(back_recv.at[pl.ds(0, ranks - 1)], send_sems.at[7])
    drain(final_recv.at[pl.ds(0, ranks - 1)], send_sems.at[8])
    drain(whole_recv.at[pl.ds(0, (ranks - 1) * n_col)], send_sems.at[9])
    conclude(child_w, 0, 0, c)
    conclude(child_w, 0, 1, c)
    conclude(child_w, 0, 2, across)
    conclude(off_w, 1, 0, c)
    conclude(off_w, 1, 1, c)
    conclude(off_w, 1, 2, across)

    @pl.when(x == 0)
    def _():
        drain(pass_buf.at[pl.ds(0, (rows_all - 1) * n_col)], send_sems.at[4])
        drain(known_send.at[pl.ds(0, 2 * rows_all - 1)], send_sems.at[5])
        drain(extra_send.at[pl.ds(0, 2 * rows_all - 1)], send_sems.at[6])
        conclude(root_w, 2, 1, c)
        conclude(root_w, 2, 2, across)

    @pl.when(x == 1)
    def _():
        drain(rr_send, send_sems.at[2])
        conclude(root_w, 2, 0, c)


def place_kernel(*refs):
    copies = [
        pltpu.make_async_copy(refs[k], refs[3 + k], refs[6].at[k]) for k in range(3)
    ]
    for copy in copies:
        copy.start()
    for copy in copies:
        copy.wait()


def fused(
    rhs_root, rhs_child, subtree_update, inv_root, inv_child, off_child, child_map, subtree_map
):
    n_col = lax.axis_size("col")
    n_row = lax.axis_size("row")
    n_leaf = lax.axis_size("leaf")
    panel = rhs_child.shape[0]
    sep = rhs_child.shape[2]
    ranks = n_row * (n_leaf // 2)
    rows_all = n_leaf * n_row
    group = 2 * ranks
    root_width = inv_root.shape[2]
    child_width = inv_child.shape[2]
    sep_blocks = child_width * n_col // BLOCK_ROWS
    root_blocks = root_width * n_col // BLOCK_ROWS
    piece = n_col * sep
    mixed = n_col + piece // BLOCK_ROWS

    vmem = pl.BlockSpec(memory_space=pltpu.VMEM)
    hbm = pl.BlockSpec(memory_space=pl.ANY)
    buffer = lambda *shape: pltpu.VMEM(shape, BF16)
    outs = pl.pallas_call(
        solve_kernel,
        out_shape=(
            jax.ShapeDtypeStruct((panel, n_col, sep), F32),
            jax.ShapeDtypeStruct((panel, n_col, sep), F32),
            jax.ShapeDtypeStruct((panel, n_col, BLOCK_ROWS), BF16),
        ),
        in_specs=[hbm] * 8,
        out_specs=(vmem, vmem, vmem),
        scratch_shapes=[
            pltpu.SMEM(child_map.shape, jnp.int32), pltpu.SMEM(subtree_map.shape, jnp.int32),
            buffer(*subtree_update.shape), buffer(*rhs_child.shape), buffer(*rhs_root.shape),
            buffer(n_col, *inv_root.shape), buffer(n_col, *inv_child.shape),
            buffer(n_col, *off_child.shape),
            buffer(2, n_col + 2, panel, BLOCK_ROWS),
            buffer(group * (n_col + 2) + 1, panel, BLOCK_ROWS),
            buffer(panel, piece), buffer(2 * rows_all, panel, piece),
            buffer(2, 2, 2 * panel, sep), buffer(group, 2, 2 * panel, sep),
            buffer(n_col + 2, panel, BLOCK_ROWS), buffer(n_col + 2, panel, BLOCK_ROWS),
            pltpu.VMEM((2, n_col, panel, BLOCK_ROWS), F32), buffer(n_col, panel, sep),
            buffer(n_col, panel, BLOCK_ROWS), buffer(2 * rows_all * n_col + 1, panel, BLOCK_ROWS),
            pltpu.VMEM((n_col, 2 * panel, root_width), F32),
            buffer(root_blocks, 2 * panel, BLOCK_ROWS),
            buffer(2 * rows_all, n_col, panel, BLOCK_ROWS),
            buffer(rows_all, n_col, panel, BLOCK_ROWS),
            buffer(2 * rows_all, piece // BLOCK_ROWS, panel, BLOCK_ROWS),
            buffer(rows_all, piece // BLOCK_ROWS, panel, BLOCK_ROWS),
            buffer(n_col, panel, BLOCK_ROWS), buffer(ranks * n_col, panel, BLOCK_ROWS),
            buffer(ranks, panel, piece), buffer(ranks, panel, piece),
            buffer(sep_blocks, panel, BLOCK_ROWS),
            buffer(ranks, mixed, panel, BLOCK_ROWS), buffer(ranks, mixed, panel, BLOCK_ROWS),
            pltpu.SemaphoreType.DMA((8,)),
            pltpu.SemaphoreType.DMA((10,)),
            pltpu.SemaphoreType.DMA((10,)),
            pltpu.SemaphoreType.DMA((3, 3, 4)),
            pltpu.SemaphoreType.DMA((3, 3, 4)),
        ],
        compiler_params=pltpu.CompilerParams(
            collective_id=0, has_side_effects=True, vmem_limit_bytes=60 * 1024 * 1024
        ),
    )(
        child_map, subtree_map, subtree_update, rhs_child, rhs_root, inv_root, inv_child, off_child,
    )
    return pl.pallas_call(
        place_kernel,
        out_shape=tuple(jax.ShapeDtypeStruct(out.shape, out.dtype) for out in outs),
        in_specs=[vmem] * 3,
        out_specs=(hbm,) * 3,
        scratch_shapes=[pltpu.SemaphoreType.DMA((3,))],
    )(*outs)


def body(*arrays):
    whole_blocks = (
        lax.axis_size("leaf") == 4
        and lax.axis_size("row") == 2
        and lax.axis_size("col") == 4
        and arrays[2].shape[2] == BLOCK_ROWS
        and arrays[4].shape[2] % BLOCK_ROWS == 0
        and arrays[0].shape[0] % 16 == 0
        and arrays[0].shape[2] % 16 == 0
        and arrays[0].shape[2] <= BLOCK_ROWS
        and arrays[0].shape[1] * arrays[0].shape[2] % BLOCK_ROWS == 0
    )
    return (fused if whole_blocks else local)(*arrays)


def solution(mesh):
    in_specs = (
        P("col", None, ("leaf", "row")),
        P("col", None, ("leaf", "row")),
        P("col", None, ("leaf", "row")),
        P(None, ("leaf", "row"), "col"),
        P(None, ("leaf", "row"), "col"),
        P(None, ("leaf", "row"), "col"),
        P(),
        P(),
    )
    out_specs = (
        P("col", None, ("leaf", "row")),
        P("col", None, ("leaf", "row")),
        P("col", None, ("leaf", "row")),
    )
    return jax.shard_map(body, mesh=mesh, in_specs=in_specs, out_specs=out_specs, check_vma=False)
```
